256 devices in a mesh: level: 32 (over y_lo, z, core), band: 8 (over x, y_hi).
Axes of the slice: x: 4, y: 4 (y_hi: 2, y_lo: 2; y = y_hi * 2 + y_lo), z: 8, core: 2. Of those that a mesh axis runs over, the one named last changes fastest.
Arguments:
- latents: float32 [32, 4, 40, 64], P('level', None, 'band'), may hold values from -18 to 18
- timesteps: int32 [32], P('level'), may hold values from 16 to 999
- fresh: float32 [1, 4, 40, 64], P(None, None, 'band'), may hold values from -6 to 6
- w_in: float32 [4, 320], replicated, may hold values from -3 to 3
- conv_first: float32 [3, 3, 320, 320], replicated, may hold values from -0.109375 to 0.109375
- conv_second: float32 [3, 3, 320, 320], replicated, may hold values from -0.109375 to 0.109375
- w_time: float32 [320, 320], replicated, may hold values from -0.3125 to 0.3125
- temporal: float32 [3, 320, 320], replicated, may hold values from -0.1875 to 0.1875
- w_out: float32 [320, 4], replicated, may hold values from -0.3125 to 0.3125
Outputs:
- queue: float32 [32, 4, 40, 64], P('level', None, 'band')
The draws below stay inside these ranges and needn't reach their ends.
All inputs are finite; a program needn't handle non-finite values.
Results may differ from the reference program's by a relative error of at most 0.0001.
Values sent between devices are 32-bit elements; how exact they have to be, the bound alone decides.
No kernel may reach another device: no remote copies, remote signals or barrier semaphores. Data moves between devices by JAX's collectives and lax.ppermute only.
A program may use at most 128 MiB of HBM per device.

```python
import math
import jax
import jax.numpy as jnp
from jax import lax

C = 320
LAT = 4
W = 64
GROUPS = 32
ITERS = 2
NSTEPS = 1000
STRIDE = 16
H = 40
LEVELS = 32


def draw_latents(key, part):
    basis_key = jax.random.fold_in(jax.random.fold_in(key, 11), 0)
    row_scale = 1.0 + 2.0 * jnp.arange(H, dtype=jnp.float32) / max(H - 1, 1)
    basis = jnp.clip(jax.random.normal(basis_key, (LEVELS, LAT, H, W), jnp.float32), -6.0, 6.0)
    return (basis * row_scale[None, None, :, None]).astype(jnp.float32)


def touch_ends(entries, stream_key, smallest, largest):
    spot = [jax.random.randint(jax.random.fold_in(stream_key, axis), (), 0, length) for axis, length in enumerate(entries.shape)]
    widest = entries.shape.index(max(entries.shape))
    neighbour = spot[:widest] + [(spot[widest] + 1) % entries.shape[widest]] + spot[widest + 1:]
    return entries.at[tuple(spot)].set(smallest).at[tuple(neighbour)].set(largest)


def levels(key, extent, cuts, smallest, largest):
    loudness = 1.0
    for dim, shards_of in cuts:
        heights = jax.random.uniform(jax.random.fold_in(jax.random.fold_in(key, 6), dim), (shards_of,), jnp.float32, smallest / len(cuts), largest / len(cuts))
        loudness = loudness * jnp.repeat(jnp.exp(heights), extent[dim] // shards_of).reshape((-1,) + (1,) * (len(extent) - 1 - dim))
    return loudness


def scatter_about(rng, shape, width, reach, cuts=(), kind=jnp.bfloat16):
    values = width * jax.random.normal(rng, shape, jnp.float32)
    if cuts:
        values = values * levels(rng, shape, cuts, -0.22, 0.18)
    return jnp.clip(values, -reach, reach).astype(kind)


def setup_inputs(seed: int = 0) -> dict:
    splits = jax.random.split(jax.random.key(seed), 10)
    latents = draw_latents(jax.random.fold_in(splits[9], 71), 0)
    timesteps = touch_ends(jax.random.randint(splits[1], (LEVELS,), STRIDE, NSTEPS), jax.random.fold_in(splits[1], 1), STRIDE, NSTEPS - 1).astype(jnp.int32)
    fresh = scatter_about(splits[2], (ITERS - 1, LAT, H, W), 1.0, 6.0, ((2, 8),), jnp.float32)
    w_in = scatter_about(splits[3], (LAT, C), LAT ** -0.5, 3.0, (), jnp.float32)
    conv_first = scatter_about(splits[4], (3, 3, C, C), (9 * C) ** -0.5, 0.109375, (), jnp.float32)
    conv_second = scatter_about(splits[5], (3, 3, C, C), (9 * C) ** -0.5, 0.109375, (), jnp.float32)
    w_time = scatter_about(splits[6], (C, C), C ** -0.5, 0.3125, (), jnp.float32)
    temporal = scatter_about(splits[7], (3, C, C), (3 * C) ** -0.5, 0.1875, (), jnp.float32)
    w_out = scatter_about(splits[8], (C, LAT), C ** -0.5, 0.3125, (), jnp.float32)
    return dict(latents=latents, timesteps=timesteps, fresh=fresh, w_in=w_in, conv_first=conv_first, conv_second=conv_second, w_time=w_time, temporal=temporal, w_out=w_out)


EPSILON = 1e-05
HIGHEST = lax.Precision.HIGHEST

def noise_table():
    position = jnp.arange(NSTEPS, dtype=jnp.float32)
    root_beta = math.sqrt(0.00085) + position / (NSTEPS - 1) * (math.sqrt(0.012) - math.sqrt(0.00085))
    return jnp.cumprod(1.0 - root_beta * root_beta)

def time_embed(step_ids, w_time):
    half_width = w_time.shape[0] // 2
    frequency = jnp.exp(-math.log(10000.0) * jnp.arange(half_width, dtype=jnp.float32) / half_width)
    angles = step_ids.astype(jnp.float32)[:, None] * frequency[None, :]
    harmonic = jnp.concatenate([jnp.cos(angles), jnp.sin(angles)], axis=1)
    return jax.nn.silu(jnp.dot(harmonic, w_time, precision=HIGHEST, preferred_element_type=jnp.float32))

def group_norm(values):
    shape_full = values.shape
    grouped = values.reshape(shape_full[0], shape_full[1], shape_full[2], GROUPS, shape_full[3] // GROUPS)
    center = lax.optimization_barrier(jnp.mean(grouped, axis=(1, 2, 4), keepdims=True))
    spread = lax.optimization_barrier(jnp.mean(grouped * grouped, axis=(1, 2, 4), keepdims=True)) - center * center
    return ((grouped - center) * lax.rsqrt(spread + EPSILON)).reshape(shape_full)

def convolve(values, kernel):
    height = values.shape[1]
    columns = values.shape[2]
    widened = jnp.pad(values, ((0, 0), (1, 1), (1, 1), (0, 0)))
    result = jnp.zeros(values.shape[:3] + (kernel.shape[3],), jnp.float32)
    for row_tap in range(3):
        for col_tap in range(3):
            result = result + jnp.einsum('lhwc,cd->lhwd', widened[:, row_tap:row_tap + height, col_tap:col_tap + columns], kernel[row_tap, col_tap], precision=HIGHEST)
    return result

def reference(latents, timesteps, fresh, w_in, conv_first, conv_second, w_time, temporal, w_out):
    levels_all = latents.shape[0]
    latent_now = latents.transpose(0, 2, 3, 1)
    plan = noise_table()
    alpha_now = plan[timesteps.astype(jnp.int32)][:, None, None, None]
    alpha_prev = plan[(timesteps - STRIDE).astype(jnp.int32)][:, None, None, None]
    embedded = time_embed(timesteps, w_time)
    for iteration in range(ITERS):
        lifted = jnp.einsum('lhwk,kc->lhwc', latent_now, w_in, precision=HIGHEST)
        middle = convolve(jax.nn.silu(group_norm(lifted)), conv_first) + embedded[:, None, None, :]
        hidden = lifted + convolve(jax.nn.silu(group_norm(middle)), conv_second)
        activated = jax.nn.silu(group_norm(hidden))
        padded = jnp.pad(activated, ((1, 1), (0, 0), (0, 0), (0, 0)))
        blended = hidden
        for tap_index in range(3):
            blended = blended + jnp.einsum('lhwc,cd->lhwd', padded[tap_index:tap_index + levels_all], temporal[tap_index], precision=HIGHEST)
        noise_pred = jnp.einsum('lhwc,ck->lhwk', blended, w_out, precision=HIGHEST)
        denoised = (latent_now - jnp.sqrt(1.0 - alpha_now) * noise_pred) / jnp.sqrt(alpha_now)
        latent_now = jnp.sqrt(alpha_prev) * denoised + jnp.sqrt(1.0 - alpha_prev) * noise_pred
        if iteration + 1 < ITERS:
            entering = fresh[iteration].transpose(1, 2, 0)[None]
            latent_now = jnp.concatenate([entering, latent_now[:-1]], axis=0)
    return latent_now.transpose(0, 3, 1, 2)
```

```python
import functools
import math

import jax
import jax.numpy as jnp
import numpy as np
from jax import lax
from jax.experimental import pallas as pl
from jax.experimental.pallas import tpu as pltpu
from jax.sharding import PartitionSpec as P

GROUPS = 32
ITERS = 2
NSTEPS = 1000
STRIDE = 16

EPSILON = 1e-05
HIGHEST = lax.Precision.HIGHEST
BF16 = jnp.bfloat16
F32 = jnp.float32


def noise_plan():
    position = np.arange(NSTEPS, dtype=np.float64)
    root_beta = math.sqrt(0.00085) + position / (NSTEPS - 1) * (
        math.sqrt(0.012) - math.sqrt(0.00085)
    )
    return np.cumprod(1.0 - root_beta * root_beta).astype(np.float32)


def time_embed(step_ids, w_time):
    half_width = w_time.shape[0] // 2
    frequency = jnp.exp(-math.log(10000.0) * jnp.arange(half_width, dtype=F32) / half_width)
    angles = step_ids.astype(F32)[:, None] * frequency[None, :]
    harmonic = jnp.concatenate([jnp.cos(angles), jnp.sin(angles)], axis=1)
    return jax.nn.silu(jnp.dot(harmonic, w_time, precision=HIGHEST, preferred_element_type=F32))


def halves(v):
    hi = v.astype(BF16)
    return hi, (v - hi.astype(F32)).astype(BF16)


def thirds(v):
    one = v.astype(BF16).astype(F32)
    two = (v - one).astype(BF16).astype(F32)
    three = ((v - one) - two).astype(BF16).astype(F32)
    return one, two, three


def silu(v):
    return v / (1.0 + jnp.exp(-v))


def group_mean(rows):
    channels = rows.shape[1]
    per_group = channels // GROUPS
    one, two, three = thirds(rows)
    stacked = jnp.concatenate([one, two, three, one * 0.0], axis=0).astype(BF16)
    shape = (channels, channels)
    factor = (1 << 16) // per_group + 1
    here = (lax.broadcasted_iota(jnp.int32, shape, 0) * factor) >> 16
    there = (lax.broadcasted_iota(jnp.int32, shape, 1) * factor) >> 16
    member = jnp.where(here == there, 1.0, 0.0).astype(BF16)
    total = jnp.dot(stacked, member, preferred_element_type=F32)
    return (total[0:2] + total[2:4] + total[4:6]) * (1.0 / per_group)


def center_factor(means):
    grouped = group_mean(means)
    center = grouped[0:1]
    return center, lax.rsqrt(grouped[1:2] - center * center + EPSILON)


def lift(frame, w):
    f1, f2, f3 = thirds(frame)
    w1, w2, w3 = thirds(w)
    left = jnp.concatenate([f1, f1, f2, f1, f2, f3], axis=0).astype(BF16)
    right = jnp.concatenate([w1, w2, w1, w3, w2, w1], axis=0).astype(BF16)
    return lax.dot_general(left, right, (((0,), (0,)), ((), ())), preferred_element_type=F32)


def put_left(a_ref, rows, act):
    hi, lo = halves(act)
    a_ref[rows, 0:256] = hi[:, 0:256]
    a_ref[rows, 256:512] = lo[:, 0:256]
    a_ref[rows, 512:768] = hi[:, 0:256]
    a_ref[rows, 768:896] = jnp.concatenate([hi[:, 256:320], lo[:, 256:320]], axis=1)
    a_ref[rows, 896:960] = hi[:, 256:320]


def put_right(b_ref, w_ref):
    for k in range(5):
        hi, lo = zip(*[halves(w_ref[0, c, 64 * k : 64 * k + 64, :]) for c in range(3)])
        if k < 4:
            places = ((64 * k, hi), (256 + 64 * k, hi), (512 + 64 * k, lo))
        else:
            places = ((768, hi), (832, hi), (896, lo))
        for at, part in places:
            for c in range(3):
                b_ref[at : at + 64, 256 * c : 256 * c + 256] = part[c][:, 0:256]
            b_ref[at : at + 64, 768:896] = jnp.concatenate(
                [part[0][:, 256:320], part[1][:, 256:320]], axis=1
            )
            b_ref[at : at + 64, 896:960] = part[2][:, 256:320]


def accumulate(acc_ref, a_ref, b_ref, tap, count):
    left = a_ref[pl.ds(pl.multiple_of(tap * 64, 64), count), :]
    for n, (lo, hi) in enumerate(((0, 256), (256, 512), (512, 768), (768, 960))):
        part = jnp.dot(left, b_ref[:, lo:hi], preferred_element_type=F32)

        @pl.when(tap == 0)
        def _():
            acc_ref[8 : 8 + count, lo:hi] = part

        @pl.when(tap > 0)
        def _():
            acc_ref[8 : 8 + count, lo:hi] += part


def shifted_sum(acc_ref, row):
    base = 8 + 64 * row
    column = lax.broadcasted_iota(jnp.int32, (64, 1), 0)
    first = column > 0
    last = column < 63
    main = (
        jnp.where(first, acc_ref[base - 1 : base + 63, 0:256], 0.0)
        + acc_ref[base : base + 64, 256:512]
        + jnp.where(last, acc_ref[base + 1 : base + 65, 512:768], 0.0)
    )
    rest = (
        jnp.where(first, acc_ref[base - 1 : base + 63, 768:832], 0.0)
        + acc_ref[base : base + 64, 832:896]
        + jnp.where(last, acc_ref[base + 1 : base + 65, 896:960], 0.0)
    )
    return jnp.concatenate([main, rest], axis=1)


def conv1_kernel(
    members, band_ref, frame_ref, w_in_ref, emb_ref, w_ref, mid_ref, stat_ref, a_ref, b_ref,
    acc_ref, lift_ref,
):
    tap = pl.program_id(0)
    band = band_ref[0]
    bands = frame_ref.shape[0]

    @pl.when(tap == 0)
    def _():
        frame = frame_ref[...]
        w = w_in_ref[...]
        average = 1.0 / members
        mean = jnp.sum(jnp.sum(frame, axis=0), axis=1, keepdims=True) * average
        mean = jnp.sum(mean * w, axis=0, keepdims=True)
        square = jnp.zeros_like(mean)
        for j in range(4):
            moment = jnp.sum(frame * frame[:, j : j + 1, :], axis=0)
            moment = jnp.sum(moment, axis=1, keepdims=True) * average
            square += w[j : j + 1] * jnp.sum(moment * w, axis=0, keepdims=True)
        center, factor = center_factor(jnp.concatenate([mean, square], axis=0))
        before = frame_ref[jnp.maximum(band - 1, 0)]
        after = frame_ref[jnp.minimum(band + 1, bands - 1)]
        around = jnp.concatenate(
            [before[:, 192:320], frame_ref[band], after[:, 0:128]], axis=1
        )
        lift_ref[...] = lift(around, w)
        for i in range(9):
            rows = slice(64 * i, 64 * i + 64)
            act = silu((lift_ref[rows, :] - center) * factor)
            if i < 2:
                act = act * jnp.where(band > 0, 1.0, 0.0)
            elif i >= 7:
                act = act * jnp.where(band < bands - 1, 1.0, 0.0)
            put_left(a_ref, rows, act)

    put_right(b_ref, w_ref)
    accumulate(acc_ref, a_ref, b_ref, tap, 448)

    @pl.when(tap == 2)
    def _():
        total = jnp.zeros((8, 320), F32)
        square = jnp.zeros((8, 320), F32)
        for i in range(7):
            out = shifted_sum(acc_ref, i) + emb_ref[...]
            mid_ref[64 * i : 64 * i + 64, :] = out
            if 1 <= i <= 5:
                folded = out.reshape(8, 8, 320)
                total += jnp.sum(folded, axis=0)
                square += jnp.sum(folded * folded, axis=0)
        stat_ref[...] = jnp.broadcast_to(
            jnp.concatenate(
                [jnp.sum(total, axis=0, keepdims=True), jnp.sum(square, axis=0, keepdims=True)],
                axis=0,
            )[None],
            stat_ref.shape,
        )


def conv2_kernel(
    members, band_ref, mid_ref, sums_ref, own_ref, w_in_ref, w_ref, hid_ref, stat_ref, a_ref,
    b_ref, acc_ref,
):
    tap = pl.program_id(0)
    band = band_ref[0]
    bands = sums_ref.shape[0]

    @pl.when(tap == 0)
    def _():
        center, factor = center_factor(jnp.sum(sums_ref[...], axis=0) * (1.0 / members))
        for i in range(7):
            rows = slice(64 * i, 64 * i + 64)
            act = silu((mid_ref[rows, :] - center) * factor)
            if i == 0:
                act = act * jnp.where(band > 0, 1.0, 0.0)
            elif i == 6:
                act = act * jnp.where(band < bands - 1, 1.0, 0.0)
            put_left(a_ref, rows, act)

    put_right(b_ref, w_ref)
    accumulate(acc_ref, a_ref, b_ref, tap, 320)

    @pl.when(tap == 2)
    def _():
        total = jnp.zeros((8, 320), F32)
        square = jnp.zeros((8, 320), F32)
        hid_ref[...] = lift(own_ref[...], w_in_ref[...])
        for i in range(5):
            rows = slice(64 * i, 64 * i + 64)
            out = hid_ref[rows, :] + shifted_sum(acc_ref, i)
            hid_ref[rows, :] = out
            folded = out.reshape(8, 8, 320)
            total += jnp.sum(folded, axis=0)
            square += jnp.sum(folded * folded, axis=0)
        stat_ref[...] = jnp.broadcast_to(
            jnp.concatenate(
                [jnp.sum(total, axis=0, keepdims=True), jnp.sum(square, axis=0, keepdims=True)],
                axis=0,
            )[None],
            stat_ref.shape,
        )


def project_kernel(members, coef_ref, hid_ref, sums_ref, own_ref, w_out_ref, fold_ref, out_ref):
    center, factor = center_factor(jnp.sum(sums_ref[...], axis=0) * (1.0 / members))
    hidden = hid_ref[...]
    act = silu((hidden - center) * factor)
    dims = (((1,), (1,)), ((), ()))
    h_hi, h_lo = halves(hidden)
    a_hi, a_lo = halves(act)
    w_hi, w_lo = halves(w_out_ref[...])
    f_hi, f_lo = halves(fold_ref[...])

    def product(l_hi, l_lo, r_hi, r_lo):
        both = lax.dot_general(
            jnp.concatenate([l_hi, l_lo], axis=0), r_hi, dims, preferred_element_type=F32
        )
        n = l_hi.shape[0]
        return (
            both[0:n] + both[n:]
            + lax.dot_general(l_hi, r_lo, dims, preferred_element_type=F32)
        )

    from_hidden = product(w_hi, w_lo, h_hi, h_lo)
    from_act = product(f_hi, f_lo, a_hi, a_lo)
    local = from_hidden[0:4] + from_act[0:4]
    out_ref[0:4] = coef_ref[0] * own_ref[...] + coef_ref[1] * local
    out_ref[4:8] = from_act[4:8]
    out_ref[8:12] = from_act[8:12]
    out_ref[12:16] = jnp.full((4, out_ref.shape[1]), coef_ref[1], F32)


SMEM = functools.partial(pl.BlockSpec, memory_space=pltpu.SMEM)
LIMIT = 40 * 1024 * 1024


def whole(*shape):
    return pl.BlockSpec(shape, lambda *_: (0,) * len(shape))


def conv_call(kernel, operands, specs, rows_in, rows_out, extra, name):
    weights = pl.BlockSpec((1, 3, 320, 320), lambda r: (r, 0, 0, 0))
    flops = 2 * rows_out * 64 * 2880 * 320
    return pl.pallas_call(
        kernel,
        grid=(3,),
        in_specs=[*specs, weights],
        out_specs=[whole(rows_out * 64, 320), whole(8, 2, 320)],
        out_shape=[
            jax.ShapeDtypeStruct((rows_out * 64, 320), F32),
            jax.ShapeDtypeStruct((8, 2, 320), F32),
        ],
        scratch_shapes=[
            pltpu.VMEM((rows_in * 64, 960), BF16),
            pltpu.VMEM((960, 960), BF16),
            pltpu.VMEM((rows_out * 64 + 16, 960), F32),
            *extra,
        ],
        compiler_params=pltpu.CompilerParams(
            dimension_semantics=("arbitrary",), vmem_limit_bytes=LIMIT
        ),
        cost_estimate=pl.CostEstimate(
            flops=3 * flops, bytes_accessed=4_000_000, transcendentals=rows_in * 64 * 320
        ),
        name=name,
    )(*operands)


def gather_bands(piece):
    size = lax.axis_size("band")
    return lax.all_to_all(
        jnp.broadcast_to(piece[None], (size, *piece.shape)), "band", 0, 0, tiled=True
    )


def on_device(latents, timesteps, fresh, w_in, conv_first, conv_second, w_time, temporal, w_out):
    bands = lax.axis_size("band")
    levels = lax.axis_size("level")
    positions = latents.shape[2] * latents.shape[3]
    frame_positions = float(positions * bands)
    level = lax.axis_index("level")
    band = lax.axis_index("band").astype(jnp.int32).reshape(1)

    own = latents[0].reshape(4, positions)
    frame = gather_bands(own)

    plan = jnp.asarray(noise_plan())
    step = timesteps[0]
    now = lax.dynamic_index_in_dim(plan, step, keepdims=False)
    prev = lax.dynamic_index_in_dim(plan, step - STRIDE, keepdims=False)
    ratio = jnp.sqrt(prev) / jnp.sqrt(now)
    coef = jnp.stack([ratio, jnp.sqrt(1.0 - prev) - ratio * jnp.sqrt(1.0 - now)])
    embedded = time_embed(timesteps, w_time)
    folded = jnp.einsum("kcd,dj->kjc", temporal, w_out, precision=HIGHEST)
    folded = jnp.concatenate([folded[1], folded[0], folded[2], jnp.zeros_like(folded[0])], axis=0)
    out_rows = jnp.concatenate([w_out.T, jnp.zeros_like(w_out.T)], axis=0)

    for iteration in range(ITERS):
        middle, stats = conv_call(
            functools.partial(conv1_kernel, frame_positions),
            (band, frame, w_in, embedded, conv_first),
            [SMEM(), whole(8, 4, 320), whole(4, 320), whole(1, 320)],
            9, 7, [pltpu.VMEM((576, 320), F32)], "conv_one",
        )
        sums = lax.all_to_all(stats, "band", 0, 0, tiled=True)
        hidden, stats = conv_call(
            functools.partial(conv2_kernel, frame_positions),
            (band, middle, sums, own, w_in, conv_second),
            [SMEM(), whole(448, 320), whole(8, 2, 320), whole(4, 320), whole(4, 320)],
            7, 5, [], "conv_two",
        )
        sums = lax.all_to_all(stats, "band", 0, 0, tiled=True)
        parts = pl.pallas_call(
            functools.partial(project_kernel, frame_positions),
            in_specs=[SMEM()] + [pl.BlockSpec(memory_space=pltpu.VMEM)] * 5,
            out_specs=pl.BlockSpec(memory_space=pltpu.VMEM),
            out_shape=jax.ShapeDtypeStruct((16, positions), F32),
            compiler_params=pltpu.CompilerParams(vmem_limit_bytes=LIMIT),
            name="project",
        )(coef, hidden, sums, own, out_rows, folded)
        if iteration + 1 < ITERS:
            inside = [(i, i + 1) for i in range(0, levels, 2)]
            across = [(i, i + 2) for i in range(1, levels - 2, 2)]
            back = [(i + 1, i) for i in range(0, levels, 2)]
            from_zero = lax.ppermute(parts, "level", inside)
            over = jnp.concatenate([parts[0:8], parts[12:16], from_zero[4:8]], axis=0)
            from_chip = lax.ppermute(over, "level", across)
            handed = lax.ppermute(
                jnp.concatenate([from_chip[0:4], from_chip[8:16]], axis=0), "level", back
            )
            odd = level % 2 == 1
            update = jnp.where(odd, from_zero[0:4], handed[0:4])
            noise = jnp.where(odd, from_zero[12:16], handed[4:8])
            below = jnp.where(odd, from_chip[4:8], handed[8:12])
            moved = update + noise * (below + parts[8:12])
            own = jnp.where(level == 0, fresh[iteration].reshape(4, positions), moved)
            frame = gather_bands(own)
        else:
            up = [(i, i + 1) for i in range(levels - 1)]
            down = [(j, i) for i, j in up]
            below = lax.ppermute(parts[4:8], "level", up)
            above = lax.ppermute(parts[8:12], "level", down)
            own = parts[0:4] + parts[12:16] * (below + above)
    return own.reshape(latents.shape)


def solution(mesh):
    placed = (
        P("level", None, "band", None),
        P("level"),
        P(None, None, "band", None),
        P(),
        P(),
        P(),
        P(),
        P(),
        P(),
    )
    return jax.shard_map(
        on_device,
        mesh=mesh,
        in_specs=placed,
        out_specs=P("level", None, "band", None),
        check_vma=False,
    )
```

```python
import functools
import math

import jax
import jax.numpy as jnp
import numpy as np
from jax import lax
from jax.experimental import pallas as pl
from jax.experimental.pallas import tpu as pltpu
from jax.sharding import PartitionSpec as P

GROUPS = 32
ITERS = 2
NSTEPS = 1000
STRIDE = 16

EPSILON = 1e-05
HIGHEST = lax.Precision.HIGHEST
BF16 = jnp.bfloat16
F32 = jnp.float32


def noise_plan():
    position = np.arange(NSTEPS, dtype=np.float64)
    root_beta = math.sqrt(0.00085) + position / (NSTEPS - 1) * (
        math.sqrt(0.012) - math.sqrt(0.00085)
    )
    return np.cumprod(1.0 - root_beta * root_beta).astype(np.float32)


def harmonics(step_ids, width):
    half_width = width // 2
    frequency = jnp.exp(-math.log(10000.0) * jnp.arange(half_width, dtype=F32) / half_width)
    angles = step_ids.astype(F32)[:, None] * frequency[None, :]
    return jnp.concatenate([jnp.cos(angles), jnp.sin(angles)], axis=1)


def halves(v):
    hi = v.astype(BF16)
    return hi, (v - hi.astype(F32)).astype(BF16)


def thirds(v):
    one = v.astype(BF16).astype(F32)
    two = (v - one).astype(BF16).astype(F32)
    three = ((v - one) - two).astype(BF16).astype(F32)
    return one, two, three


def silu(v):
    return v / (1.0 + jnp.exp(-v))


def group_mean(rows):
    channels = rows.shape[1]
    per_group = channels // GROUPS
    one, two, three = thirds(rows)
    stacked = jnp.concatenate([one, two, three, one * 0.0], axis=0).astype(BF16)
    shape = (channels, channels)
    factor = (1 << 16) // per_group + 1
    here = (lax.broadcasted_iota(jnp.int32, shape, 0) * factor) >> 16
    there = (lax.broadcasted_iota(jnp.int32, shape, 1) * factor) >> 16
    member = jnp.where(here == there, 1.0, 0.0).astype(BF16)
    total = jnp.dot(stacked, member, preferred_element_type=F32)
    return (total[0:2] + total[2:4] + total[4:6]) * (1.0 / per_group)


def center_factor(means):
    grouped = group_mean(means)
    center = grouped[0:1]
    return center, lax.rsqrt(grouped[1:2] - center * center + EPSILON)


def lift(frame, w):
    f1, f2, f3 = thirds(frame)
    w1, w2, w3 = thirds(w)
    left = jnp.concatenate([f1, f1, f2, f1, f2, f3], axis=0).astype(BF16)
    right = jnp.concatenate([w1, w2, w1, w3, w2, w1], axis=0).astype(BF16)
    return lax.dot_general(left, right, (((0,), (0,)), ((), ())), preferred_element_type=F32)


def put_left(a_ref, rows, act):
    hi, lo = halves(act)
    a_ref[rows, 0:256] = hi[:, 0:256]
    a_ref[rows, 256:512] = lo[:, 0:256]
    a_ref[rows, 512:768] = hi[:, 0:256]
    a_ref[rows, 768:896] = jnp.concatenate([hi[:, 256:320], lo[:, 256:320]], axis=1)
    a_ref[rows, 896:1024] = jnp.concatenate([hi[:, 256:320], hi[:, 256:320] * 0.0], axis=1)


def put_right(b_ref, tap, w_ref):
    for k in range(5):
        hi, lo = zip(*[halves(w_ref[c, 64 * k : 64 * k + 64, :]) for c in range(3)])
        if k < 4:
            places = ((64 * k, hi), (256 + 64 * k, hi), (512 + 64 * k, lo))
        else:
            places = ((768, hi), (832, hi), (896, lo))
        for at, part in places:
            for c in range(3):
                b_ref[tap, at : at + 64, 256 * c : 256 * c + 256] = part[c][:, 0:256]
            b_ref[tap, at : at + 64, 768:896] = jnp.concatenate(
                [part[0][:, 256:320], part[1][:, 256:320]], axis=1
            )
            b_ref[tap, at : at + 64, 896:960] = part[2][:, 256:320]
    b_ref[tap, 960:1024, :] = jnp.zeros((64, 960), BF16)


def product(left, right, dims):
    l_hi, l_lo = halves(left)
    r_hi, r_lo = halves(right)
    n = left.shape[0]
    both = lax.dot_general(
        jnp.concatenate([l_hi, l_lo], axis=0), r_hi, (dims, ((), ())), preferred_element_type=F32
    )
    rest = lax.dot_general(l_hi, r_lo, (dims, ((), ())), preferred_element_type=F32)
    return both[0:n] + both[n:] + rest


def spread_kernel(
    steps_ref, latents_ref, harmonic_ref, spread_ref, own_ref, step_ref
):
    own = jnp.concatenate([latents_ref[0, r] for r in range(5)], axis=1)
    own_ref[...] = own
    spread_ref[...] = jnp.broadcast_to(own[None], spread_ref.shape)
    step_ref[...] = jnp.full(step_ref.shape, steps_ref[0].astype(F32), F32)


def setup_kernel(
    after_ref, step_ref, plan_ref, fresh_ref, harmonic_ref, w_out_ref, time_ref, temporal_ref,
    one_ref, two_ref, new_ref, coef_ref, emb_ref, fold_ref, first_ref, second_ref,
):
    new_ref[...] = jnp.concatenate([fresh_ref[0, r] for r in range(5)], axis=1)
    step = step_ref[...].astype(jnp.int32)
    plan = plan_ref[...]
    place = lax.broadcasted_iota(jnp.int32, plan.shape, 0) * 128 + lax.broadcasted_iota(
        jnp.int32, plan.shape, 1
    )

    def at(i):
        return jnp.sum(
            jnp.sum(jnp.where(place == i, plan, 0.0), axis=0, keepdims=True), axis=1, keepdims=True
        )

    now = at(step)
    prev = at(step - STRIDE)
    ratio = jnp.sqrt(prev) / jnp.sqrt(now)
    noise = jnp.sqrt(1.0 - prev) - ratio * jnp.sqrt(1.0 - now)
    coef_ref[0:1] = jnp.broadcast_to(ratio, (1, 128))
    coef_ref[1:2] = jnp.broadcast_to(noise, (1, 128))
    for raw, ref in ((one_ref, first_ref), (two_ref, second_ref)):
        for r in range(3):
            put_right(ref, r, raw.at[r])
    harmonic = jnp.broadcast_to(harmonic_ref[...], (8, 320))
    emb_ref[...] = silu(product(harmonic, time_ref[...], ((1,), (0,)))[0:1])
    w_out = jnp.concatenate([w_out_ref[...], w_out_ref[...] * 0.0], axis=0)
    for row, tap in enumerate((1, 0, 2)):
        fold = product(w_out, temporal_ref[tap], ((1,), (1,)))
        fold_ref[4 * row : 4 * row + 4] = fold[0:4]
    fold_ref[12:16] = jnp.zeros((4, 320), F32)


def setup(*operands):
    shapes = (
        ((4, 320), F32), ((2, 128), F32), ((1, 320), F32), ((16, 320), F32),
        ((3, 1024, 960), BF16), ((3, 1024, 960), BF16),
    )
    return pl.pallas_call(
        setup_kernel,
        in_specs=[ANY] + [VMEM] * (len(operands) - 1),
        out_specs=[VMEM] * len(shapes),
        out_shape=[jax.ShapeDtypeStruct(*shape) for shape in shapes],
        compiler_params=pltpu.CompilerParams(vmem_limit_bytes=LIMIT),
        cost_estimate=pl.CostEstimate(flops=0, bytes_accessed=20_000_000, transcendentals=0),
        name="setup",
    )(*operands)


def multiply(acc_ref, a_ref, b_ref, count):
    left = jnp.concatenate([a_ref[64 * tap : 64 * tap + count, :] for tap in range(3)], axis=1)
    for lo, hi in ((0, 256), (256, 512), (512, 768), (768, 960)):
        right = jnp.concatenate([b_ref[tap, :, lo:hi] for tap in range(3)], axis=0)
        acc_ref[8 : 8 + count, lo:hi] = jnp.dot(left, right, preferred_element_type=F32)


def shifted_sum(acc_ref, row):
    base = 8 + 64 * row
    column = lax.broadcasted_iota(jnp.int32, (64, 1), 0)
    first = column > 0
    last = column < 63
    main = (
        jnp.where(first, acc_ref[base - 1 : base + 63, 0:256], 0.0)
        + acc_ref[base : base + 64, 256:512]
        + jnp.where(last, acc_ref[base + 1 : base + 65, 512:768], 0.0)
    )
    rest = (
        jnp.where(first, acc_ref[base - 1 : base + 63, 768:832], 0.0)
        + acc_ref[base : base + 64, 832:896]
        + jnp.where(last, acc_ref[base + 1 : base + 65, 896:960], 0.0)
    )
    return jnp.concatenate([main, rest], axis=1)


def conv1_kernel(
    members, frame_ref, w_in_ref, emb_ref, w_ref, mid_ref, stat_ref, a_ref, acc_ref,
    lift_ref,
):
    band = lax.axis_index("band")
    bands = frame_ref.shape[0]

    frame = frame_ref[...]
    w = w_in_ref[...]
    average = 1.0 / members
    mean = jnp.sum(jnp.sum(frame, axis=0), axis=1, keepdims=True) * average
    mean = jnp.sum(mean * w, axis=0, keepdims=True)
    square = jnp.zeros_like(mean)
    for j in range(4):
        moment = jnp.sum(frame * frame[:, j : j + 1, :], axis=0)
        moment = jnp.sum(moment, axis=1, keepdims=True) * average
        square += w[j : j + 1] * jnp.sum(moment * w, axis=0, keepdims=True)
    center, factor = center_factor(jnp.concatenate([mean, square], axis=0))
    before = frame_ref[jnp.maximum(band - 1, 0)]
    after = frame_ref[jnp.minimum(band + 1, bands - 1)]
    around = jnp.concatenate(
        [before[:, 192:320], frame_ref[band], after[:, 0:128]], axis=1
    )
    lift_ref[...] = lift(around, w)
    for i in range(9):
        rows = slice(64 * i, 64 * i + 64)
        act = silu((lift_ref[rows, :] - center) * factor)
        if i < 2:
            act = act * jnp.where(band > 0, 1.0, 0.0)
        elif i >= 7:
            act = act * jnp.where(band < bands - 1, 1.0, 0.0)
        put_left(a_ref, rows, act)

    multiply(acc_ref, a_ref, w_ref, 448)

    total = jnp.zeros((8, 320), F32)
    square = jnp.zeros((8, 320), F32)
    for i in range(7):
        out = shifted_sum(acc_ref, i) + emb_ref[...]
        mid_ref[64 * i : 64 * i + 64, :] = out
        if 1 <= i <= 5:
            folded = out.reshape(8, 8, 320)
            total += jnp.sum(folded, axis=0)
            square += jnp.sum(folded * folded, axis=0)
    stat_ref[...] = jnp.broadcast_to(
        jnp.concatenate(
            [jnp.sum(total, axis=0, keepdims=True), jnp.sum(square, axis=0, keepdims=True)],
            axis=0,
        )[None],
        stat_ref.shape,
    )


def conv2_kernel(
    members, mid_ref, sums_ref, own_ref, w_in_ref, w_ref, hid_ref, stat_ref, a_ref,
    acc_ref,
):
    band = lax.axis_index("band")
    bands = sums_ref.shape[0]

    center, factor = center_factor(jnp.sum(sums_ref[...], axis=0) * (1.0 / members))
    for i in range(7):
        rows = slice(64 * i, 64 * i + 64)
        act = silu((mid_ref[rows, :] - center) * factor)
        if i == 0:
            act = act * jnp.where(band > 0, 1.0, 0.0)
        elif i == 6:
            act = act * jnp.where(band < bands - 1, 1.0, 0.0)
        put_left(a_ref, rows, act)

    multiply(acc_ref, a_ref, w_ref, 320)

    total = jnp.zeros((8, 320), F32)
    square = jnp.zeros((8, 320), F32)
    hid_ref[...] = lift(own_ref[...], w_in_ref[...])
    for i in range(5):
        rows = slice(64 * i, 64 * i + 64)
        out = hid_ref[rows, :] + shifted_sum(acc_ref, i)
        hid_ref[rows, :] = out
        folded = out.reshape(8, 8, 320)
        total += jnp.sum(folded, axis=0)
        square += jnp.sum(folded * folded, axis=0)
    stat_ref[...] = jnp.broadcast_to(
        jnp.concatenate(
            [jnp.sum(total, axis=0, keepdims=True), jnp.sum(square, axis=0, keepdims=True)],
            axis=0,
        )[None],
        stat_ref.shape,
    )


def project_kernel(members, hid_ref, sums_ref, own_ref, w_out_ref, fold_ref, coef_ref, out_ref):
    center, factor = center_factor(jnp.sum(sums_ref[...], axis=0) * (1.0 / members))
    hidden = hid_ref[...]
    act = silu((hidden - center) * factor)
    w_out = jnp.concatenate([w_out_ref[...], w_out_ref[...] * 0.0], axis=0)
    from_hidden = product(w_out, hidden, ((1,), (1,)))
    from_act = product(fold_ref[...], act, ((1,), (1,)))
    local = from_hidden[0:4] + from_act[0:4]
    ratio = coef_ref[0:1, 0:1]
    noise = coef_ref[1:2, 0:1]
    out_ref[0:4] = ratio * own_ref[...] + noise * local
    out_ref[4:8] = from_act[4:8]
    out_ref[8:12] = from_act[8:12]
    out_ref[12:16] = jnp.broadcast_to(noise, (4, out_ref.shape[1]))


def merge_kernel(parts_ref, zero_ref, chip_ref, handed_ref, fresh_ref, own_ref, spread_ref):
    level = lax.axis_index("level")
    odd = jnp.where(level % 2 == 1, 1.0, 0.0)
    even = 1.0 - odd
    new = jnp.where(level == 0, 1.0, 0.0)
    update = odd * zero_ref[0:4] + even * handed_ref[0:4]
    noise = odd * zero_ref[12:16] + even * handed_ref[4:8]
    below = odd * chip_ref[4:8] + even * handed_ref[8:12]
    moved = update + noise * (below + parts_ref[8:12])
    own = new * fresh_ref[...] + (1.0 - new) * moved
    own_ref[...] = own
    spread_ref[...] = jnp.broadcast_to(own[None], spread_ref.shape)


def finish_kernel(parts_ref, below_ref, above_ref, out_ref):
    own = parts_ref[0:4] + parts_ref[12:16] * (below_ref[...] + above_ref[...])
    for r in range(5):
        out_ref[0, r] = own[:, 64 * r : 64 * r + 64]


SMEM = pl.BlockSpec(memory_space=pltpu.SMEM)
VMEM = pl.BlockSpec(memory_space=pltpu.VMEM)
ANY = pl.BlockSpec(memory_space=pl.ANY)
LIMIT = 20 * 1024 * 1024


def conv_call(kernel, operands, rows_in, rows_out, extra, name):
    return pl.pallas_call(
        kernel,
        in_specs=[VMEM] * len(operands),
        out_specs=[VMEM, VMEM],
        out_shape=[
            jax.ShapeDtypeStruct((rows_out * 64, 320), F32),
            jax.ShapeDtypeStruct((8, 2, 320), F32),
        ],
        scratch_shapes=[
            pltpu.VMEM((rows_in * 64, 1024), BF16),
            pltpu.VMEM((rows_out * 64 + 16, 960), F32),
            *extra,
        ],
        compiler_params=pltpu.CompilerParams(vmem_limit_bytes=LIMIT),
        cost_estimate=pl.CostEstimate(
            flops=6 * rows_out * 64 * 2880 * 320,
            bytes_accessed=4_000_000,
            transcendentals=rows_in * 64 * 320,
        ),
        name=name,
    )(*operands)


def call(kernel, in_specs, shapes, operands, name, cost=None):
    return pl.pallas_call(
        kernel,
        in_specs=in_specs,
        out_specs=[VMEM] * len(shapes),
        out_shape=[jax.ShapeDtypeStruct(shape, F32) for shape in shapes],
        compiler_params=pltpu.CompilerParams(vmem_limit_bytes=LIMIT),
        cost_estimate=cost,
        name=name,
    )(*operands)


def on_device(latents, timesteps, fresh, w_in, conv_first, conv_second, w_time, temporal, w_out):
    levels = lax.axis_size("level")
    positions = latents.shape[2] * latents.shape[3]
    members = float(positions * lax.axis_size("band"))
    out_rows = w_out.T
    harmonic = harmonics(timesteps, w_time.shape[0])
    plan = np.zeros((8, 128), np.float32)
    plan.reshape(-1)[:NSTEPS] = noise_plan()
    plan = jnp.asarray(plan)
    spread, own, step = call(
        spread_kernel, [SMEM, VMEM, ANY], [(8, 4, positions), (4, positions), (1, 128)],
        (timesteps, latents.transpose(0, 2, 1, 3), harmonic), "spread",
        pl.CostEstimate(flops=8_000_000_000, bytes_accessed=40_000, transcendentals=0),
    )
    for iteration in range(ITERS):
        frame = lax.all_to_all(spread, "band", 0, 0, tiled=True)
        if iteration == 0:
            new, coef, embedded, folded, first_ready, second_ready = setup(
                frame, step, plan, fresh.transpose(0, 2, 1, 3), harmonic, out_rows, w_time,
                temporal, conv_first, conv_second,
            )
        middle, stats = conv_call(
            functools.partial(conv1_kernel, members),
            (frame, w_in, embedded, first_ready),
            9, 7, [pltpu.VMEM((576, 320), F32)], "conv_one",
        )
        sums = lax.all_to_all(stats, "band", 0, 0, tiled=True)
        hidden, stats = conv_call(
            functools.partial(conv2_kernel, members),
            (middle, sums, own, w_in, second_ready),
            7, 5, [], "conv_two",
        )
        sums = lax.all_to_all(stats, "band", 0, 0, tiled=True)
        (parts,) = call(
            functools.partial(project_kernel, members), [VMEM] * 6, [(16, positions)],
            (hidden, sums, own, out_rows, folded, coef), "project",
        )
        if iteration + 1 < ITERS:
            inside = [(i, i + 1) for i in range(0, levels, 2)]
            across = [(i, i + 2) for i in range(1, levels - 2, 2)]
            back = [(i + 1, i) for i in range(0, levels, 2)]
            from_zero = lax.ppermute(parts, "level", inside)
            over = jnp.concatenate([parts[0:8], parts[12:16], from_zero[4:8]], axis=0)
            from_chip = lax.ppermute(over, "level", across)
            handed = lax.ppermute(
                jnp.concatenate([from_chip[0:4], from_chip[8:16]], axis=0), "level", back
            )
            own, spread = call(
                merge_kernel, [VMEM] * 5, [(4, positions), spread.shape],
                (parts, from_zero, from_chip, handed, new), "merge",
            )
        else:
            up = [(i, i + 1) for i in range(levels - 1)]
            down = [(j, i) for i, j in up]
            below = lax.ppermute(parts[4:8], "level", up)
            above = lax.ppermute(parts[8:12], "level", down)
            (out,) = call(
                finish_kernel, [VMEM] * 3, [(1, 5, 4, 64)], (parts, below, above), "finish"
            )
    return out.transpose(0, 2, 1, 3)


def solution(mesh):
    placed = (
        P("level", None, "band", None),
        P("level"),
        P(None, None, "band", None),
        P(),
        P(),
        P(),
        P(),
        P(),
        P(),
    )
    return jax.shard_map(
        on_device,
        mesh=mesh,
        in_specs=placed,
        out_specs=P("level", None, "band", None),
        check_vma=False,
    )
```

```python
import functools
import math

import jax
import jax.numpy as jnp
import numpy as np
from jax import lax
from jax.experimental import pallas as pl
from jax.experimental.pallas import tpu as pltpu
from jax.sharding import PartitionSpec as P

GROUPS = 32
ITERS = 2
NSTEPS = 1000
STRIDE = 16

EPSILON = 1e-05
HIGHEST = lax.Precision.HIGHEST
BF16 = jnp.bfloat16
F32 = jnp.float32


def noise_plan():
    position = np.arange(NSTEPS, dtype=np.float64)
    root_beta = math.sqrt(0.00085) + position / (NSTEPS - 1) * (
        math.sqrt(0.012) - math.sqrt(0.00085)
    )
    return np.cumprod(1.0 - root_beta * root_beta).astype(np.float32)


def harmonics(step_ids, width):
    half_width = width // 2
    frequency = jnp.exp(-math.log(10000.0) * jnp.arange(half_width, dtype=F32) / half_width)
    angles = step_ids.astype(F32)[:, None] * frequency[None, :]
    return jnp.concatenate([jnp.cos(angles), jnp.sin(angles)], axis=1)


def halves(v):
    hi = v.astype(BF16)
    return hi, (v - hi.astype(F32)).astype(BF16)


def thirds(v):
    one = v.astype(BF16).astype(F32)
    two = (v - one).astype(BF16).astype(F32)
    three = ((v - one) - two).astype(BF16).astype(F32)
    return one, two, three


def silu(v):
    return v / (1.0 + jnp.exp(-v))


def group_mean(rows):
    channels = rows.shape[1]
    per_group = channels // GROUPS
    one, two, three = thirds(rows)
    stacked = jnp.concatenate([one, two, three, one * 0.0], axis=0).astype(BF16)
    shape = (channels, channels)
    factor = (1 << 16) // per_group + 1
    here = (lax.broadcasted_iota(jnp.int32, shape, 0) * factor) >> 16
    there = (lax.broadcasted_iota(jnp.int32, shape, 1) * factor) >> 16
    member = jnp.where(here == there, 1.0, 0.0).astype(BF16)
    total = jnp.dot(stacked, member, preferred_element_type=F32)
    return (total[0:2] + total[2:4] + total[4:6]) * (1.0 / per_group)


def center_factor(means):
    grouped = group_mean(means)
    center = grouped[0:1]
    return center, lax.rsqrt(grouped[1:2] - center * center + EPSILON)


def lift(frame, w):
    f1, f2, f3 = thirds(frame)
    w1, w2, w3 = thirds(w)
    left = jnp.concatenate([f1, f1, f2, f1, f2, f3], axis=0).astype(BF16)
    right = jnp.concatenate([w1, w2, w1, w3, w2, w1], axis=0).astype(BF16)
    return lax.dot_general(left, right, (((0,), (0,)), ((), ())), preferred_element_type=F32)


def put_left(a_ref, rows, act):
    hi, lo = halves(act)
    a_ref[rows, 0:256] = hi[:, 0:256]
    a_ref[rows, 256:512] = lo[:, 0:256]
    a_ref[rows, 512:768] = hi[:, 0:256]
    a_ref[rows, 768:896] = jnp.concatenate([hi[:, 256:320], lo[:, 256:320]], axis=1)
    a_ref[rows, 896:1024] = jnp.concatenate([hi[:, 256:320], hi[:, 256:320] * 0.0], axis=1)


def put_right(b_ref, tap, w_ref):
    for k in range(5):
        hi, lo = zip(*[halves(w_ref[c, 64 * k : 64 * k + 64, :]) for c in range(3)])
        if k < 4:
            places = ((64 * k, hi), (256 + 64 * k, hi), (512 + 64 * k, lo))
        else:
            places = ((768, hi), (832, hi), (896, lo))
        for at, part in places:
            for c in range(3):
                b_ref[tap, at : at + 64, 256 * c : 256 * c + 256] = part[c][:, 0:256]
            b_ref[tap, at : at + 64, 768:896] = jnp.concatenate(
                [part[0][:, 256:320], part[1][:, 256:320]], axis=1
            )
            b_ref[tap, at : at + 64, 896:960] = part[2][:, 256:320]
    b_ref[tap, 960:1024, :] = jnp.zeros((64, 960), BF16)


def product(left, right, dims):
    l_hi, l_lo = halves(left)
    r_hi, r_lo = halves(right)
    n = left.shape[0]
    both = lax.dot_general(
        jnp.concatenate([l_hi, l_lo], axis=0), r_hi, (dims, ((), ())), preferred_element_type=F32
    )
    rest = lax.dot_general(l_hi, r_lo, (dims, ((), ())), preferred_element_type=F32)
    return both[0:n] + both[n:] + rest


def spread_kernel(
    steps_ref, latents_ref, fresh_ref, harmonic_ref, spread_ref, step_ref
):
    rows = [
        jnp.concatenate([ref[0, r] for r in range(5)], axis=1) for ref in (latents_ref, fresh_ref)
    ]
    both = jnp.concatenate(rows, axis=0)
    spread_ref[...] = jnp.broadcast_to(both[None], spread_ref.shape)
    step_ref[...] = jnp.full(step_ref.shape, steps_ref[0].astype(F32), F32)


def setup_kernel(
    frame_ref, step_ref, plan_ref, harmonic_ref, w_out_ref, time_ref, temporal_ref, one_ref,
    two_ref, own_ref, before_ref, after_ref, across_ref, new_ref, coef_ref, emb_ref, fold_ref,
    first_ref, second_ref,
):
    strip = lax.axis_index("band") >> 1

    def piece(ahead, row):
        at = 2 * ((strip + ahead) & 3)
        return jnp.concatenate(
            [frame_ref[at, row : row + 4, :], frame_ref[at + 1, row : row + 4, :]], axis=1
        )

    for ref, ahead in ((own_ref, 0), (before_ref, 3), (after_ref, 1), (across_ref, 2)):
        ref[...] = piece(ahead, 0)
    new_ref[...] = piece(0, 4)
    step = step_ref[...].astype(jnp.int32)
    plan = plan_ref[...]
    place = lax.broadcasted_iota(jnp.int32, plan.shape, 0) * 128 + lax.broadcasted_iota(
        jnp.int32, plan.shape, 1
    )

    def at(i):
        return jnp.sum(
            jnp.sum(jnp.where(place == i, plan, 0.0), axis=0, keepdims=True), axis=1, keepdims=True
        )

    now = at(step)
    prev = at(step - STRIDE)
    ratio = jnp.sqrt(prev) / jnp.sqrt(now)
    noise = jnp.sqrt(1.0 - prev) - ratio * jnp.sqrt(1.0 - now)
    coef_ref[0:1] = jnp.broadcast_to(ratio, (1, 128))
    coef_ref[1:2] = jnp.broadcast_to(noise, (1, 128))
    for raw, ref in ((one_ref, first_ref), (two_ref, second_ref)):
        for r in range(3):
            put_right(ref, r, raw.at[r])
    harmonic = jnp.broadcast_to(harmonic_ref[...], (8, 320))
    emb_ref[...] = silu(product(harmonic, time_ref[...], ((1,), (0,)))[0:1])
    w_out = jnp.concatenate([w_out_ref[...], w_out_ref[...] * 0.0], axis=0)
    for row, tap in enumerate((1, 0, 2)):
        fold = product(w_out, temporal_ref[tap], ((1,), (1,)))
        fold_ref[4 * row : 4 * row + 4] = fold[0:4]
    fold_ref[12:16] = jnp.zeros((4, 320), F32)


def setup(*operands):
    shapes = (
        *[((4, 640), F32)] * 5, ((2, 128), F32), ((1, 320), F32), ((16, 320), F32),
        ((3, 1024, 960), BF16), ((3, 1024, 960), BF16),
    )
    return pl.pallas_call(
        setup_kernel,
        in_specs=[VMEM] * len(operands),
        out_specs=[VMEM] * len(shapes),
        out_shape=[jax.ShapeDtypeStruct(*shape) for shape in shapes],
        compiler_params=pltpu.CompilerParams(vmem_limit_bytes=LIMIT),
        cost_estimate=pl.CostEstimate(flops=0, bytes_accessed=20_000_000, transcendentals=0),
        name="setup",
    )(*operands)


def multiply(acc_ref, a_ref, b_ref, count):
    left = jnp.concatenate([a_ref[64 * tap : 64 * tap + count, :] for tap in range(3)], axis=1)
    for lo, hi in ((0, 256), (256, 512), (512, 768), (768, 960)):
        right = jnp.concatenate([b_ref[tap, :, lo:hi] for tap in range(3)], axis=0)
        acc_ref[8 : 8 + count, lo:hi] = jnp.dot(left, right, preferred_element_type=F32)


def shifted_sum(acc_ref, row):
    base = 8 + 64 * row
    column = lax.broadcasted_iota(jnp.int32, (64, 1), 0)
    first = column > 0
    last = column < 63
    main = (
        jnp.where(first, acc_ref[base - 1 : base + 63, 0:256], 0.0)
        + acc_ref[base : base + 64, 256:512]
        + jnp.where(last, acc_ref[base + 1 : base + 65, 512:768], 0.0)
    )
    rest = (
        jnp.where(first, acc_ref[base - 1 : base + 63, 768:832], 0.0)
        + acc_ref[base : base + 64, 832:896]
        + jnp.where(last, acc_ref[base + 1 : base + 65, 896:960], 0.0)
    )
    return jnp.concatenate([main, rest], axis=1)


def write_sums(stat_ref, total, square):
    stat_ref[...] = jnp.concatenate(
        [jnp.sum(total, axis=0, keepdims=True), jnp.sum(square, axis=0, keepdims=True)], axis=0
    )


def conv1_kernel(
    members, own_ref, before_ref, after_ref, across_ref, w_in_ref, emb_ref, w_ref, mid_ref, stat_ref,
    a_ref, acc_ref, lift_ref,
):
    strip = lax.axis_index("band") >> 1
    pieces = [ref[...] for ref in (own_ref, before_ref, after_ref, across_ref)]
    w = w_in_ref[...]
    average = 1.0 / members
    mean = jnp.sum(sum(pieces), axis=1, keepdims=True) * average
    mean = jnp.sum(mean * w, axis=0, keepdims=True)
    square = jnp.zeros_like(mean)
    for j in range(4):
        moment = sum(piece * piece[j : j + 1] for piece in pieces)
        moment = jnp.sum(moment, axis=1, keepdims=True) * average
        square += w[j : j + 1] * jnp.sum(moment * w, axis=0, keepdims=True)
    center, factor = center_factor(jnp.concatenate([mean, square], axis=0))
    around = jnp.concatenate([pieces[1][:, 512:640], pieces[0], pieces[2][:, 0:128]], axis=1)
    lift_ref[...] = lift(around, w)
    for i in range(14):
        rows = slice(64 * i, 64 * i + 64)
        act = silu((lift_ref[rows, :] - center) * factor)
        if i < 2:
            act = act * jnp.where(strip > 0, 1.0, 0.0)
        elif i >= 12:
            act = act * jnp.where(strip < 3, 1.0, 0.0)
        put_left(a_ref, rows, act)
    multiply(acc_ref, a_ref, w_ref, 768)
    total = jnp.zeros((8, 320), F32)
    square = jnp.zeros((8, 320), F32)
    for i in range(12):
        out = shifted_sum(acc_ref, i) + emb_ref[...]
        mid_ref[64 * i : 64 * i + 64, :] = out
        if 1 <= i <= 10:
            folded = out.reshape(8, 8, 320)
            total += jnp.sum(folded, axis=0)
            square += jnp.sum(folded * folded, axis=0)
    write_sums(stat_ref, total, square)


def conv2_kernel(
    members, mid_ref, sum0_ref, sum1_ref, sum2_ref, sum3_ref, own_ref, w_in_ref, w_ref, hid_ref,
    stat_ref, a_ref, acc_ref,
):
    strip = lax.axis_index("band") >> 1
    sums = sum0_ref[...] + sum1_ref[...] + sum2_ref[...] + sum3_ref[...]
    center, factor = center_factor(sums * (1.0 / members))
    for i in range(12):
        rows = slice(64 * i, 64 * i + 64)
        act = silu((mid_ref[rows, :] - center) * factor)
        if i == 0:
            act = act * jnp.where(strip > 0, 1.0, 0.0)
        elif i == 11:
            act = act * jnp.where(strip < 3, 1.0, 0.0)
        put_left(a_ref, rows, act)
    multiply(acc_ref, a_ref, w_ref, 640)
    total = jnp.zeros((8, 320), F32)
    square = jnp.zeros((8, 320), F32)
    hid_ref[...] = lift(own_ref[...], w_in_ref[...])
    for i in range(10):
        rows = slice(64 * i, 64 * i + 64)
        out = hid_ref[rows, :] + shifted_sum(acc_ref, i)
        hid_ref[rows, :] = out
        folded = out.reshape(8, 8, 320)
        total += jnp.sum(folded, axis=0)
        square += jnp.sum(folded * folded, axis=0)
    write_sums(stat_ref, total, square)


def project_kernel(
    members, last, hid_ref, sum0_ref, sum1_ref, sum2_ref, sum3_ref, own_ref, w_out_ref, fold_ref,
    coef_ref, out_ref,
):
    sums = sum0_ref[...] + sum1_ref[...] + sum2_ref[...] + sum3_ref[...]
    center, factor = center_factor(sums * (1.0 / members))
    if last:
        low = lax.axis_index("band") & 1
        hidden = hid_ref[pl.ds(pl.multiple_of(low * 320, 64), 320), :]
        both = own_ref[...]
        own = jnp.where(low == 0, both[:, 0:320], both[:, 320:640])
    else:
        hidden = hid_ref[...]
        own = own_ref[...]
    act = silu((hidden - center) * factor)
    w_out = jnp.concatenate([w_out_ref[...], w_out_ref[...] * 0.0], axis=0)
    from_hidden = product(w_out, hidden, ((1,), (1,)))
    from_act = product(fold_ref[...], act, ((1,), (1,)))
    local = from_hidden[0:4] + from_act[0:4]
    ratio = coef_ref[0:1, 0:1]
    noise = coef_ref[1:2, 0:1]
    out_ref[0:4] = ratio * own + noise * local
    out_ref[4:8] = jnp.broadcast_to(noise, (4, out_ref.shape[1]))
    out_ref[8:12] = from_act[4:8]
    out_ref[12:16] = from_act[8:12]


def merge_kernel(parts_ref, one_ref, two_ref, fresh_ref, own_ref):
    moved = one_ref[0:4] + one_ref[4:8] * (two_ref[...] + parts_ref[12:16])
    own_ref[...] = jnp.where(lax.axis_index("level") == 0, fresh_ref[...], moved)


def finish_kernel(parts_ref, below_ref, above_ref, out_ref):
    own = parts_ref[0:4] + parts_ref[4:8] * (below_ref[...] + above_ref[...])
    for r in range(5):
        out_ref[0, r] = own[:, 64 * r : 64 * r + 64]


SMEM = pl.BlockSpec(memory_space=pltpu.SMEM)
VMEM = pl.BlockSpec(memory_space=pltpu.VMEM)
ANY = pl.BlockSpec(memory_space=pl.ANY)
LIMIT = 20 * 1024 * 1024


def conv_call(kernel, operands, rows_in, rows_out, extra, name):
    return pl.pallas_call(
        kernel,
        in_specs=[VMEM] * len(operands),
        out_specs=[VMEM, VMEM],
        out_shape=[
            jax.ShapeDtypeStruct((rows_out * 64, 320), F32),
            jax.ShapeDtypeStruct((2, 320), F32),
        ],
        scratch_shapes=[
            pltpu.VMEM((rows_in * 64, 1024), BF16),
            pltpu.VMEM((rows_out * 64 + 16, 960), F32),
            *extra,
        ],
        compiler_params=pltpu.CompilerParams(vmem_limit_bytes=LIMIT),
        cost_estimate=pl.CostEstimate(
            flops=6 * rows_out * 64 * 2880 * 320,
            bytes_accessed=4_000_000,
            transcendentals=rows_in * 64 * 320,
        ),
        name=name,
    )(*operands)


def call(kernel, in_specs, shapes, operands, name, cost=None):
    return pl.pallas_call(
        kernel,
        in_specs=in_specs,
        out_specs=[VMEM] * len(shapes),
        out_shape=[jax.ShapeDtypeStruct(shape, F32) for shape in shapes],
        compiler_params=pltpu.CompilerParams(vmem_limit_bytes=LIMIT),
        cost_estimate=cost,
        name=name,
    )(*operands)


def around_strip(value):
    bands = lax.axis_size("band")
    return [value] + [
        lax.ppermute(value, "band", [(i, (i + 2 * k) % bands) for i in range(bands)])
        for k in (1, 3, 2)
    ]


def on_device(latents, timesteps, fresh, w_in, conv_first, conv_second, w_time, temporal, w_out):
    levels = lax.axis_size("level")
    positions = latents.shape[2] * latents.shape[3]
    members = float(positions * lax.axis_size("band"))
    out_rows = w_out.T
    harmonic = harmonics(timesteps, w_time.shape[0])
    plan = np.zeros((8, 128), np.float32)
    plan.reshape(-1)[:NSTEPS] = noise_plan()
    plan = jnp.asarray(plan)
    spread, step = call(
        spread_kernel, [SMEM, VMEM, VMEM, ANY], [(8, 8, positions), (1, 128)],
        (timesteps, latents.transpose(0, 2, 1, 3), fresh.transpose(0, 2, 1, 3), harmonic),
        "spread", pl.CostEstimate(flops=8_000_000_000, bytes_accessed=40_000, transcendentals=0),
    )
    frame = lax.all_to_all(spread, "band", 0, 0, tiled=True)
    *pieces, new, coef, embedded, folded, first_ready, second_ready = setup(
        frame, step, plan, harmonic, out_rows, w_time, temporal, conv_first, conv_second
    )
    for iteration in range(ITERS):
        last = iteration + 1 == ITERS
        middle, stats = conv_call(
            functools.partial(conv1_kernel, members),
            (*pieces, w_in, embedded, first_ready),
            14, 12, [pltpu.VMEM((896, 320), F32)], "conv_one",
        )
        hidden, stats = conv_call(
            functools.partial(conv2_kernel, members),
            (middle, *around_strip(stats), pieces[0], w_in, second_ready),
            12, 10, [], "conv_two",
        )
        width = positions if last else 2 * positions
        (parts,) = call(
            functools.partial(project_kernel, members, last), [VMEM] * 9, [(16, width)],
            (hidden, *around_strip(stats), pieces[0], out_rows, folded, coef), "project",
        )
        if last:
            up = [(i, i + 1) for i in range(levels - 1)]
            down = [(j, i) for i, j in up]
            below = lax.ppermute(parts[8:12], "level", up)
            above = lax.ppermute(parts[12:16], "level", down)
            (out,) = call(
                finish_kernel, [VMEM] * 3, [(1, 5, 4, 64)], (parts, below, above), "finish"
            )
        else:
            one = lax.ppermute(parts[0:8], "level", [(i, i + 1) for i in range(levels - 1)])
            two = lax.ppermute(parts[8:12], "level", [(i, i + 2) for i in range(levels - 2)])
            (own,) = call(
                merge_kernel, [VMEM] * 4, [(4, width)], (parts, one, two, new), "merge"
            )
            pieces = around_strip(own)
    return out.transpose(0, 2, 1, 3)


def solution(mesh):
    placed = (
        P("level", None, "band", None),
        P("level"),
        P(None, None, "band", None),
        P(),
        P(),
        P(),
        P(),
        P(),
        P(),
    )
    return jax.shard_map(
        on_device,
        mesh=mesh,
        in_specs=placed,
        out_specs=P("level", None, "band", None),
        check_vma=False,
    )
```

```python
import functools
import math

import jax
import jax.numpy as jnp
import numpy as np
from jax import lax
from jax.experimental import pallas as pl
from jax.experimental.pallas import tpu as pltpu
from jax.sharding import PartitionSpec as P

GROUPS = 32
ITERS = 2
NSTEPS = 1000
STRIDE = 16

EPSILON = 1e-05
HIGHEST = lax.Precision.HIGHEST
BF16 = jnp.bfloat16
F32 = jnp.float32


def noise_plan():
    position = np.arange(NSTEPS, dtype=np.float64)
    root_beta = math.sqrt(0.00085) + position / (NSTEPS - 1) * (
        math.sqrt(0.012) - math.sqrt(0.00085)
    )
    return np.cumprod(1.0 - root_beta * root_beta).astype(np.float32)


def harmonics(step_ids, width):
    half_width = width // 2
    frequency = jnp.exp(-math.log(10000.0) * jnp.arange(half_width, dtype=F32) / half_width)
    angles = step_ids.astype(F32)[:, None] * frequency[None, :]
    return jnp.concatenate([jnp.cos(angles), jnp.sin(angles)], axis=1)


def halves(v):
    hi = v.astype(BF16)
    return hi, (v - hi.astype(F32)).astype(BF16)


def thirds(v):
    one = v.astype(BF16).astype(F32)
    two = (v - one).astype(BF16).astype(F32)
    three = ((v - one) - two).astype(BF16).astype(F32)
    return one, two, three


def silu(v):
    return v / (1.0 + jnp.exp(-v))


def group_mean(rows):
    channels = rows.shape[1]
    per_group = channels // GROUPS
    one, two, three = thirds(rows)
    stacked = jnp.concatenate([one, two, three, one * 0.0], axis=0).astype(BF16)
    shape = (channels, channels)
    factor = (1 << 16) // per_group + 1
    here = (lax.broadcasted_iota(jnp.int32, shape, 0) * factor) >> 16
    there = (lax.broadcasted_iota(jnp.int32, shape, 1) * factor) >> 16
    member = jnp.where(here == there, 1.0, 0.0).astype(BF16)
    total = jnp.dot(stacked, member, preferred_element_type=F32)
    return (total[0:2] + total[2:4] + total[4:6]) * (1.0 / per_group)


def center_factor(means):
    grouped = group_mean(means)
    center = grouped[0:1]
    return center, lax.rsqrt(grouped[1:2] - center * center + EPSILON)


def lift(frame, w):
    f1, f2, f3 = thirds(frame)
    w1, w2, w3 = thirds(w)
    left = jnp.concatenate([f1, f1, f2, f1, f2, f3], axis=0).astype(BF16)
    right = jnp.concatenate([w1, w2, w1, w3, w2, w1], axis=0).astype(BF16)
    return lax.dot_general(left, right, (((0,), (0,)), ((), ())), preferred_element_type=F32)


def put_left(a_ref, rows, act):
    hi, lo = halves(act)
    a_ref[rows, 0:256] = hi[:, 0:256]
    a_ref[rows, 256:512] = lo[:, 0:256]
    a_ref[rows, 512:768] = hi[:, 0:256]
    a_ref[rows, 768:896] = jnp.concatenate([hi[:, 256:320], lo[:, 256:320]], axis=1)
    a_ref[rows, 896:1024] = jnp.concatenate([hi[:, 256:320], hi[:, 256:320] * 0.0], axis=1)


def put_right(b_ref, tap, w_ref):
    for k in range(5):
        hi, lo = zip(*[halves(w_ref[c, 64 * k : 64 * k + 64, :]) for c in range(3)])
        if k < 4:
            places = ((64 * k, hi), (256 + 64 * k, hi), (512 + 64 * k, lo))
        else:
            places = ((768, hi), (832, hi), (896, lo))
        for at, part in places:
            for c in range(3):
                b_ref[tap, at : at + 64, 256 * c : 256 * c + 256] = part[c][:, 0:256]
            b_ref[tap, at : at + 64, 768:896] = jnp.concatenate(
                [part[0][:, 256:320], part[1][:, 256:320]], axis=1
            )
            b_ref[tap, at : at + 64, 896:960] = part[2][:, 256:320]
    b_ref[tap, 960:1024, :] = jnp.zeros((64, 960), BF16)


def product(left, right, dims):
    l_hi, l_lo = halves(left)
    r_hi, r_lo = halves(right)
    n = left.shape[0]
    both = lax.dot_general(
        jnp.concatenate([l_hi, l_lo], axis=0), r_hi, (dims, ((), ())), preferred_element_type=F32
    )
    rest = lax.dot_general(l_hi, r_lo, (dims, ((), ())), preferred_element_type=F32)
    return both[0:n] + both[n:] + rest


def spread_kernel(
    steps_ref, latents_ref, fresh_ref, harmonic_ref, spread_ref, step_ref
):
    rows = [
        jnp.concatenate([ref[0, r] for r in range(5)], axis=1) for ref in (latents_ref, fresh_ref)
    ]
    both = jnp.concatenate(rows, axis=0)
    spread_ref[...] = jnp.broadcast_to(both[None], spread_ref.shape)
    step_ref[...] = jnp.full(step_ref.shape, steps_ref[0].astype(F32), F32)


def setup_kernel(
    frame_ref, step_ref, plan_ref, harmonic_ref, time_ref, raw_ref, own_ref, flip1_ref, flip3_ref,
    flip2_ref, new_ref, coef_ref, emb_ref, first_ref,
):
    strip = lax.axis_index("band") >> 1

    def piece(flip, row):
        at = 2 * (strip ^ flip)
        return jnp.concatenate(
            [frame_ref[at, row : row + 4, :], frame_ref[at + 1, row : row + 4, :]], axis=1
        )

    for ref, flip in ((own_ref, 0), (flip1_ref, 1), (flip3_ref, 3), (flip2_ref, 2)):
        ref[...] = piece(flip, 0)
    new_ref[...] = piece(0, 4)
    step = step_ref[...].astype(jnp.int32)
    plan = plan_ref[...]
    place = lax.broadcasted_iota(jnp.int32, plan.shape, 0) * 128 + lax.broadcasted_iota(
        jnp.int32, plan.shape, 1
    )

    def at(i):
        return jnp.sum(
            jnp.sum(jnp.where(place == i, plan, 0.0), axis=0, keepdims=True), axis=1, keepdims=True
        )

    now = at(step)
    prev = at(step - STRIDE)
    ratio = jnp.sqrt(prev) / jnp.sqrt(now)
    noise = jnp.sqrt(1.0 - prev) - ratio * jnp.sqrt(1.0 - now)
    coef_ref[0:1] = jnp.broadcast_to(ratio, (1, 128))
    coef_ref[1:2] = jnp.broadcast_to(noise, (1, 128))
    for r in range(3):
        put_right(first_ref, r, raw_ref.at[r])
    harmonic = jnp.broadcast_to(harmonic_ref[...], (8, 320))
    emb_ref[...] = silu(product(harmonic, time_ref[...], ((1,), (0,)))[0:1])


def setup_second_kernel(after_ref, w_out_ref, temporal_ref, raw_ref, fold_ref, second_ref):
    for r in range(3):
        put_right(second_ref, r, raw_ref.at[r])
    w_out = jnp.concatenate([w_out_ref[...], w_out_ref[...] * 0.0], axis=0)
    for row, tap in enumerate((1, 0, 2)):
        fold = product(w_out, temporal_ref[tap], ((1,), (1,)))
        fold_ref[4 * row : 4 * row + 4] = fold[0:4]
    fold_ref[12:16] = jnp.zeros((4, 320), F32)


def setup(kernel, specs, shapes, operands, name):
    return pl.pallas_call(
        kernel,
        in_specs=specs,
        out_specs=[VMEM] * (len(shapes) + 1),
        out_shape=[
            *[jax.ShapeDtypeStruct(shape, F32) for shape in shapes],
            jax.ShapeDtypeStruct((3, 1024, 960), BF16),
        ],
        compiler_params=pltpu.CompilerParams(vmem_limit_bytes=LIMIT),
        cost_estimate=pl.CostEstimate(flops=0, bytes_accessed=10_000_000, transcendentals=0),
        name=name,
    )(*operands)


def multiply(acc_ref, a_ref, b_ref, count):
    left = jnp.concatenate([a_ref[64 * tap : 64 * tap + count, :] for tap in range(3)], axis=1)
    for lo, hi in ((0, 256), (256, 512), (512, 768), (768, 960)):
        right = jnp.concatenate([b_ref[tap, :, lo:hi] for tap in range(3)], axis=0)
        acc_ref[8 : 8 + count, lo:hi] = jnp.dot(left, right, preferred_element_type=F32)


def shifted_sum(acc_ref, row):
    base = 8 + 64 * row
    column = lax.broadcasted_iota(jnp.int32, (64, 1), 0)
    first = column > 0
    last = column < 63
    main = (
        jnp.where(first, acc_ref[base - 1 : base + 63, 0:256], 0.0)
        + acc_ref[base : base + 64, 256:512]
        + jnp.where(last, acc_ref[base + 1 : base + 65, 512:768], 0.0)
    )
    rest = (
        jnp.where(first, acc_ref[base - 1 : base + 63, 768:832], 0.0)
        + acc_ref[base : base + 64, 832:896]
        + jnp.where(last, acc_ref[base + 1 : base + 65, 896:960], 0.0)
    )
    return jnp.concatenate([main, rest], axis=1)


def write_sums(stat_ref, total, square):
    stat_ref[...] = jnp.concatenate(
        [jnp.sum(total, axis=0, keepdims=True), jnp.sum(square, axis=0, keepdims=True)], axis=0
    )


def conv1_kernel(
    members, own_ref, flip1_ref, flip3_ref, flip2_ref, w_in_ref, emb_ref, w_ref, mid_ref, stat_ref,
    a_ref, acc_ref, lift_ref,
):
    strip = lax.axis_index("band") >> 1
    pieces = [ref[...] for ref in (own_ref, flip1_ref, flip3_ref, flip2_ref)]
    w = w_in_ref[...]
    average = 1.0 / members
    mean = jnp.sum(sum(pieces), axis=1, keepdims=True) * average
    mean = jnp.sum(mean * w, axis=0, keepdims=True)
    square = jnp.zeros_like(mean)
    for j in range(4):
        moment = sum(piece * piece[j : j + 1] for piece in pieces)
        moment = jnp.sum(moment, axis=1, keepdims=True) * average
        square += w[j : j + 1] * jnp.sum(moment * w, axis=0, keepdims=True)
    center, factor = center_factor(jnp.concatenate([mean, square], axis=0))
    odd = (strip & 1) == 1
    before = jnp.where(odd, pieces[1][:, 512:640], pieces[2][:, 512:640])
    after = jnp.where(odd, pieces[2][:, 0:128], pieces[1][:, 0:128])
    around = jnp.concatenate([before, pieces[0], after], axis=1)
    lift_ref[...] = lift(around, w)
    for i in range(14):
        rows = slice(64 * i, 64 * i + 64)
        act = silu((lift_ref[rows, :] - center) * factor)
        if i < 2:
            act = act * jnp.where(strip > 0, 1.0, 0.0)
        elif i >= 12:
            act = act * jnp.where(strip < 3, 1.0, 0.0)
        put_left(a_ref, rows, act)
    multiply(acc_ref, a_ref, w_ref, 768)
    total = jnp.zeros((8, 320), F32)
    square = jnp.zeros((8, 320), F32)
    for i in range(12):
        out = shifted_sum(acc_ref, i) + emb_ref[...]
        mid_ref[64 * i : 64 * i + 64, :] = out
        if 1 <= i <= 10:
            folded = out.reshape(8, 8, 320)
            total += jnp.sum(folded, axis=0)
            square += jnp.sum(folded * folded, axis=0)
    write_sums(stat_ref, total, square)


def conv2_kernel(
    members, mid_ref, sum0_ref, sum1_ref, sum2_ref, sum3_ref, own_ref, w_in_ref, w_ref, hid_ref,
    stat_ref, a_ref, acc_ref,
):
    strip = lax.axis_index("band") >> 1
    sums = sum0_ref[...] + sum1_ref[...] + sum2_ref[...] + sum3_ref[...]
    center, factor = center_factor(sums * (1.0 / members))
    for i in range(12):
        rows = slice(64 * i, 64 * i + 64)
        act = silu((mid_ref[rows, :] - center) * factor)
        if i == 0:
            act = act * jnp.where(strip > 0, 1.0, 0.0)
        elif i == 11:
            act = act * jnp.where(strip < 3, 1.0, 0.0)
        put_left(a_ref, rows, act)
    multiply(acc_ref, a_ref, w_ref, 640)
    total = jnp.zeros((8, 320), F32)
    square = jnp.zeros((8, 320), F32)
    hid_ref[...] = lift(own_ref[...], w_in_ref[...])
    for i in range(10):
        rows = slice(64 * i, 64 * i + 64)
        out = hid_ref[rows, :] + shifted_sum(acc_ref, i)
        hid_ref[rows, :] = out
        folded = out.reshape(8, 8, 320)
        total += jnp.sum(folded, axis=0)
        square += jnp.sum(folded * folded, axis=0)
    write_sums(stat_ref, total, square)


def project_kernel(
    members, last, hid_ref, sum0_ref, sum1_ref, sum2_ref, sum3_ref, own_ref, w_out_ref, fold_ref,
    coef_ref, out_ref,
):
    sums = sum0_ref[...] + sum1_ref[...] + sum2_ref[...] + sum3_ref[...]
    center, factor = center_factor(sums * (1.0 / members))
    if last:
        low = lax.axis_index("band") & 1
        hidden = hid_ref[pl.ds(pl.multiple_of(low * 320, 64), 320), :]
        both = own_ref[...]
        own = jnp.where(low == 0, both[:, 0:320], both[:, 320:640])
    else:
        hidden = hid_ref[...]
        own = own_ref[...]
    act = silu((hidden - center) * factor)
    w_out = jnp.concatenate([w_out_ref[...], w_out_ref[...] * 0.0], axis=0)
    from_hidden = product(w_out, hidden, ((1,), (1,)))
    from_act = product(fold_ref[...], act, ((1,), (1,)))
    local = from_hidden[0:4] + from_act[0:4]
    ratio = coef_ref[0:1, 0:1]
    noise = coef_ref[1:2, 0:1]
    out_ref[0:4] = ratio * own + noise * local
    out_ref[4:8] = jnp.broadcast_to(noise, (4, out_ref.shape[1]))
    even = (lax.axis_index("level") & 1) == 0 if last else True
    out_ref[8:12] = jnp.where(even, from_act[4:8], from_act[8:12])
    out_ref[12:16] = jnp.where(even, from_act[8:12], from_act[4:8])


def merge_kernel(parts_ref, one_ref, two_ref, fresh_ref, own_ref):
    moved = one_ref[0:4] + one_ref[4:8] * (two_ref[...] + parts_ref[12:16])
    own_ref[...] = jnp.where(lax.axis_index("level") == 0, fresh_ref[...], moved)


def finish_kernel(parts_ref, core_ref, chip_ref, out_ref):
    own = parts_ref[0:4] + parts_ref[4:8] * (core_ref[...] + chip_ref[...])
    for r in range(5):
        out_ref[0, r] = own[:, 64 * r : 64 * r + 64]


SMEM = pl.BlockSpec(memory_space=pltpu.SMEM)
VMEM = pl.BlockSpec(memory_space=pltpu.VMEM)
ANY = pl.BlockSpec(memory_space=pl.ANY)
LIMIT = 20 * 1024 * 1024


def conv_call(kernel, operands, rows_in, rows_out, extra, name):
    return pl.pallas_call(
        kernel,
        in_specs=[VMEM] * len(operands),
        out_specs=[VMEM, VMEM],
        out_shape=[
            jax.ShapeDtypeStruct((rows_out * 64, 320), F32),
            jax.ShapeDtypeStruct((2, 320), F32),
        ],
        scratch_shapes=[
            pltpu.VMEM((rows_in * 64, 1024), BF16),
            pltpu.VMEM((rows_out * 64 + 16, 960), F32),
            *extra,
        ],
        compiler_params=pltpu.CompilerParams(vmem_limit_bytes=LIMIT),
        cost_estimate=pl.CostEstimate(
            flops=6 * rows_out * 64 * 2880 * 320,
            bytes_accessed=4_000_000,
            transcendentals=rows_in * 64 * 320,
        ),
        name=name,
    )(*operands)


def call(kernel, in_specs, shapes, operands, name, cost=None):
    return pl.pallas_call(
        kernel,
        in_specs=in_specs,
        out_specs=[VMEM] * len(shapes),
        out_shape=[jax.ShapeDtypeStruct(shape, F32) for shape in shapes],
        compiler_params=pltpu.CompilerParams(vmem_limit_bytes=LIMIT),
        cost_estimate=cost,
        name=name,
    )(*operands)


def around_strip(value):
    bands = lax.axis_size("band")
    return [value] + [
        lax.ppermute(value, "band", [(i, i ^ (2 * flip)) for i in range(bands)])
        for flip in (1, 3, 2)
    ]


def swap_slots(to_core, to_chip):
    levels = lax.axis_size("level")
    across = [(i, i + 1) for i in range(1, levels - 1, 2)]
    across = across + [(j, i) for i, j in across]
    from_core = lax.ppermute(to_core, "level", [(i, i ^ 1) for i in range(levels)])
    from_chip = lax.ppermute(to_chip, "level", across)
    return from_core, from_chip


def on_device(latents, timesteps, fresh, w_in, conv_first, conv_second, w_time, temporal, w_out):
    levels = lax.axis_size("level")
    positions = latents.shape[2] * latents.shape[3]
    members = float(positions * lax.axis_size("band"))
    out_rows = w_out.T
    harmonic = harmonics(timesteps, w_time.shape[0])
    plan = np.zeros((8, 128), np.float32)
    plan.reshape(-1)[:NSTEPS] = noise_plan()
    plan = jnp.asarray(plan)
    spread, step = call(
        spread_kernel, [SMEM, VMEM, VMEM, ANY], [(8, 8, positions), (1, 128)],
        (timesteps, latents.transpose(0, 2, 1, 3), fresh.transpose(0, 2, 1, 3), harmonic),
        "spread", pl.CostEstimate(flops=8_000_000_000, bytes_accessed=40_000, transcendentals=0),
    )
    frame = lax.all_to_all(spread, "band", 0, 0, tiled=True)
    *pieces, new, coef, embedded, first_ready = setup(
        setup_kernel, [VMEM] * 6, [*[(4, 2 * positions)] * 5, (2, 128), (1, 320)],
        (frame, step, plan, harmonic, w_time, conv_first), "setup_first",
    )
    for iteration in range(ITERS):
        last = iteration + 1 == ITERS
        middle, stats = conv_call(
            functools.partial(conv1_kernel, members),
            (*pieces, w_in, embedded, first_ready),
            14, 12, [pltpu.VMEM((896, 320), F32)], "conv_one",
        )
        if iteration == 0:
            folded, second_ready = setup(
                setup_second_kernel, [ANY] + [VMEM] * 3, [(16, 320)],
                (stats, out_rows, temporal, conv_second), "setup_second",
            )
        hidden, stats = conv_call(
            functools.partial(conv2_kernel, members),
            (middle, *around_strip(stats), pieces[0], w_in, second_ready),
            12, 10, [], "conv_two",
        )
        width = positions if last else 2 * positions
        (parts,) = call(
            functools.partial(project_kernel, members, last), [VMEM] * 9, [(16, width)],
            (hidden, *around_strip(stats), pieces[0], out_rows, folded, coef), "project",
        )
        if last:
            (out,) = call(
                finish_kernel, [VMEM] * 3, [(1, 5, 4, 64)],
                (parts, *swap_slots(parts[8:12], parts[12:16])), "finish",
            )
        else:
            one = lax.ppermute(parts[0:8], "level", [(i, i + 1) for i in range(levels - 1)])
            two = lax.ppermute(parts[8:12], "level", [(i, i + 2) for i in range(levels - 2)])
            (own,) = call(
                merge_kernel, [VMEM] * 4, [(4, width)], (parts, one, two, new), "merge"
            )
            pieces = around_strip(own)
    return out.transpose(0, 2, 1, 3)


def solution(mesh):
    placed = (
        P("level", None, "band", None),
        P("level"),
        P(None, None, "band", None),
        P(),
        P(),
        P(),
        P(),
        P(),
        P(),
    )
    return jax.shard_map(
        on_device,
        mesh=mesh,
        in_specs=placed,
        out_specs=P("level", None, "band", None),
        check_vma=False,
    )
```

```python
import functools
import math

import jax
import jax.numpy as jnp
import numpy as np
from jax import lax
from jax.experimental import pallas as pl
from jax.experimental.pallas import tpu as pltpu
from jax.sharding import PartitionSpec as P

GROUPS = 32
ITERS = 2
NSTEPS = 1000
STRIDE = 16

EPSILON = 1e-05
HIGHEST = lax.Precision.HIGHEST
BF16 = jnp.bfloat16
F32 = jnp.float32


def noise_plan():
    position = np.arange(NSTEPS, dtype=np.float64)
    root_beta = math.sqrt(0.00085) + position / (NSTEPS - 1) * (
        math.sqrt(0.012) - math.sqrt(0.00085)
    )
    return np.cumprod(1.0 - root_beta * root_beta).astype(np.float32)


def harmonics(step_ids, width):
    half_width = width // 2
    frequency = jnp.exp(-math.log(10000.0) * jnp.arange(half_width, dtype=F32) / half_width)
    angles = step_ids.astype(F32)[:, None] * frequency[None, :]
    return jnp.concatenate([jnp.cos(angles), jnp.sin(angles)], axis=1)


def halves(v):
    hi = v.astype(BF16)
    return hi, (v - hi.astype(F32)).astype(BF16)


def thirds(v):
    one = v.astype(BF16).astype(F32)
    two = (v - one).astype(BF16).astype(F32)
    three = ((v - one) - two).astype(BF16).astype(F32)
    return one, two, three


def silu(v):
    return v / (1.0 + jnp.exp(-v))


def group_mean(rows):
    channels = rows.shape[1]
    per_group = channels // GROUPS
    one, two, three = thirds(rows)
    stacked = jnp.concatenate([one, two, three, one * 0.0], axis=0).astype(BF16)
    shape = (channels, channels)
    factor = (1 << 16) // per_group + 1
    here = (lax.broadcasted_iota(jnp.int32, shape, 0) * factor) >> 16
    there = (lax.broadcasted_iota(jnp.int32, shape, 1) * factor) >> 16
    member = jnp.where(here == there, 1.0, 0.0).astype(BF16)
    total = jnp.dot(stacked, member, preferred_element_type=F32)
    return (total[0:2] + total[2:4] + total[4:6]) * (1.0 / per_group)


def center_factor(means):
    grouped = group_mean(means)
    center = grouped[0:1]
    return center, lax.rsqrt(grouped[1:2] - center * center + EPSILON)


def lift(frame, w):
    f1, f2, f3 = thirds(frame)
    w1, w2, w3 = thirds(w)
    left = jnp.concatenate([f1, f1, f2, f1, f2, f3], axis=0).astype(BF16)
    right = jnp.concatenate([w1, w2, w1, w3, w2, w1], axis=0).astype(BF16)
    return lax.dot_general(left, right, (((0,), (0,)), ((), ())), preferred_element_type=F32)


def put_left(a_ref, j, rows, act):
    hi, lo = halves(act)
    a_ref[j, rows, 0:256] = hi[:, 0:256]
    a_ref[j, rows, 256:512] = lo[:, 0:256]
    a_ref[j, rows, 512:768] = hi[:, 0:256]
    a_ref[j, rows, 768:896] = jnp.concatenate([hi[:, 256:320], lo[:, 256:320]], axis=1)
    a_ref[j, rows, 896:1024] = jnp.concatenate([hi[:, 256:320], hi[:, 256:320] * 0.0], axis=1)


def put_pairs(a_ref, act_ref, pairs):
    for t in range(pairs):
        d0, d1, d2, d3 = (act_ref[128 * t + 64 * i : 128 * t + 64 * i + 64, :] for i in range(4))
        for j, mixed in enumerate((d0 - d2, d1 + d2, d2 - d1, d1 - d3)):
            put_left(a_ref, j, slice(64 * t, 64 * t + 64), mixed)


def put_right(b_ref, raw_ref):
    for k in range(5):
        taps = []
        for c in range(3):
            g0, g1, g2 = (raw_ref[r, c, 64 * k : 64 * k + 64, :] for r in range(3))
            ends = (g0 + g2) * 0.5
            middle = g1 * 0.5
            taps.append((g0, ends + middle, ends - middle, g2))
        for j in range(4):
            hi, lo = zip(*[halves(tap[j]) for tap in taps])
            if k < 4:
                places = ((64 * k, hi), (256 + 64 * k, hi), (512 + 64 * k, lo))
            else:
                places = ((768, hi), (832, hi), (896, lo))
            for at, part in places:
                for c in range(3):
                    b_ref[j, at : at + 64, 256 * c : 256 * c + 256] = part[c][:, 0:256]
                b_ref[j, at : at + 64, 768:896] = jnp.concatenate(
                    [part[0][:, 256:320], part[1][:, 256:320]], axis=1
                )
                b_ref[j, at : at + 64, 896:960] = part[2][:, 256:320]
    for j in range(4):
        b_ref[j, 960:1024, :] = jnp.zeros((64, 960), BF16)


def product(left, right, dims):
    l_hi, l_lo = halves(left)
    r_hi, r_lo = halves(right)
    n = left.shape[0]
    both = lax.dot_general(
        jnp.concatenate([l_hi, l_lo], axis=0), r_hi, (dims, ((), ())), preferred_element_type=F32
    )
    rest = lax.dot_general(l_hi, r_lo, (dims, ((), ())), preferred_element_type=F32)
    return both[0:n] + both[n:] + rest


def spread_kernel(
    steps_ref, frames_ref, harmonic_ref, spread_ref, step_ref
):
    rows = [
        jnp.concatenate([frames_ref[i, r] for r in range(5)], axis=1) for i in range(2)
    ]
    both = jnp.concatenate(rows, axis=0)
    spread_ref[...] = jnp.broadcast_to(both[None], spread_ref.shape)
    step_ref[...] = jnp.full(step_ref.shape, steps_ref[0].astype(F32), F32)


def setup_kernel(
    frame_ref, step_ref, plan_ref, harmonic_ref, time_ref, raw_ref, own_ref, flip1_ref, flip3_ref,
    flip2_ref, new_ref, coef_ref, emb_ref, first_ref,
):
    strip = lax.axis_index("band") >> 1

    def piece(flip, row):
        at = 2 * (strip ^ flip)
        return jnp.concatenate(
            [frame_ref[at, row : row + 4, :], frame_ref[at + 1, row : row + 4, :]], axis=1
        )

    for ref, flip in ((own_ref, 0), (flip1_ref, 1), (flip3_ref, 3), (flip2_ref, 2)):
        ref[...] = piece(flip, 0)
    new_ref[...] = piece(0, 4)
    step = step_ref[...].astype(jnp.int32)
    plan = plan_ref[...]
    place = lax.broadcasted_iota(jnp.int32, plan.shape, 0) * 128 + lax.broadcasted_iota(
        jnp.int32, plan.shape, 1
    )

    def at(i):
        return jnp.sum(
            jnp.sum(jnp.where(place == i, plan, 0.0), axis=0, keepdims=True), axis=1, keepdims=True
        )

    now = at(step)
    prev = at(step - STRIDE)
    ratio = jnp.sqrt(prev) / jnp.sqrt(now)
    noise = jnp.sqrt(1.0 - prev) - ratio * jnp.sqrt(1.0 - now)
    coef_ref[0:1] = jnp.broadcast_to(ratio, (1, 128))
    coef_ref[1:2] = jnp.broadcast_to(noise, (1, 128))
    put_right(first_ref, raw_ref)
    harmonic = jnp.broadcast_to(harmonic_ref[...], (8, 320))
    emb_ref[...] = silu(product(harmonic, time_ref[...], ((1,), (0,)))[0:1])


def setup_second_kernel(after_ref, w_out_ref, temporal_ref, raw_ref, fold_ref, second_ref):
    put_right(second_ref, raw_ref)
    w_out = jnp.concatenate([w_out_ref[...], w_out_ref[...] * 0.0], axis=0)
    for row, tap in enumerate((1, 0, 2)):
        fold = product(w_out, temporal_ref[tap], ((1,), (1,)))
        fold_ref[4 * row : 4 * row + 4] = fold[0:4]
    fold_ref[12:16] = jnp.zeros((4, 320), F32)


def setup(kernel, specs, shapes, operands, name):
    return pl.pallas_call(
        kernel,
        in_specs=specs,
        out_specs=[VMEM] * (len(shapes) + 1),
        out_shape=[
            *[jax.ShapeDtypeStruct(shape, F32) for shape in shapes],
            jax.ShapeDtypeStruct((4, 1024, 960), BF16),
        ],
        compiler_params=pltpu.CompilerParams(vmem_limit_bytes=LIMIT),
        cost_estimate=pl.CostEstimate(flops=0, bytes_accessed=10_000_000, transcendentals=0),
        name=name,
    )(*operands)


def multiply(acc_ref, a_ref, b_ref, count):
    for j in range(4):
        for lo, hi in ((0, 256), (256, 512), (512, 768), (768, 960)):
            acc_ref[j, 8 : 8 + count, lo:hi] = jnp.dot(
                a_ref[j], b_ref[j, :, lo:hi], preferred_element_type=F32
            )


def shifted_pair(acc_ref, t):
    base = 8 + 64 * t
    column = lax.broadcasted_iota(jnp.int32, (64, 1), 0)
    first = column > 0
    last = column < 63

    def tap(shift, lo, hi):
        m1, m2, m3, m4 = (acc_ref[j, base + shift : base + shift + 64, lo:hi] for j in range(4))
        return (m1 + (m2 + m3), (m2 - m3) - m4)

    out = []
    for at, width in ((0, 256), (768, 64)):
        left = tap(-1, at, at + width)
        here = tap(0, at + width, at + 2 * width)
        right = tap(1, at + 2 * width, at + 3 * width)
        out.append(
            [
                jnp.where(first, left[i], 0.0) + here[i] + jnp.where(last, right[i], 0.0)
                for i in range(2)
            ]
        )
    return [jnp.concatenate([out[0][i], out[1][i]], axis=1) for i in range(2)]


def write_sums(stat_ref, total, square):
    stat_ref[...] = jnp.concatenate(
        [jnp.sum(total, axis=0, keepdims=True), jnp.sum(square, axis=0, keepdims=True)], axis=0
    )


def conv1_kernel(
    members, own_ref, flip1_ref, flip3_ref, flip2_ref, w_in_ref, emb_ref, w_ref, mid_ref, stat_ref,
    a_ref, acc_ref, lift_ref,
):
    strip = lax.axis_index("band") >> 1
    pieces = [ref[...] for ref in (own_ref, flip1_ref, flip3_ref, flip2_ref)]
    w = w_in_ref[...]
    average = 1.0 / members
    mean = jnp.sum(sum(pieces), axis=1, keepdims=True) * average
    mean = jnp.sum(mean * w, axis=0, keepdims=True)
    square = jnp.zeros_like(mean)
    for j in range(4):
        moment = sum(piece * piece[j : j + 1] for piece in pieces)
        moment = jnp.sum(moment, axis=1, keepdims=True) * average
        square += w[j : j + 1] * jnp.sum(moment * w, axis=0, keepdims=True)
    center, factor = center_factor(jnp.concatenate([mean, square], axis=0))
    odd = (strip & 1) == 1
    before = jnp.where(odd, pieces[1][:, 512:640], pieces[2][:, 512:640])
    after = jnp.where(odd, pieces[2][:, 0:128], pieces[1][:, 0:128])
    around = jnp.concatenate([before, pieces[0], after], axis=1)
    lift_ref[...] = lift(around, w)
    for i in range(14):
        rows = slice(64 * i, 64 * i + 64)
        act = silu((lift_ref[rows, :] - center) * factor)
        if i < 2:
            act = act * jnp.where(strip > 0, 1.0, 0.0)
        elif i >= 12:
            act = act * jnp.where(strip < 3, 1.0, 0.0)
        lift_ref[rows, :] = act
    put_pairs(a_ref, lift_ref, 6)
    multiply(acc_ref, a_ref, w_ref, 384)
    total = jnp.zeros((8, 320), F32)
    square = jnp.zeros((8, 320), F32)
    for i in range(12):
        if i % 2 == 0:
            pair = shifted_pair(acc_ref, i // 2)
        out = pair[i % 2] + emb_ref[...]
        mid_ref[64 * i : 64 * i + 64, :] = out
        if 1 <= i <= 10:
            folded = out.reshape(8, 8, 320)
            total += jnp.sum(folded, axis=0)
            square += jnp.sum(folded * folded, axis=0)
    write_sums(stat_ref, total, square)


def conv2_kernel(
    members, mid_ref, sum0_ref, sum1_ref, sum2_ref, sum3_ref, own_ref, w_in_ref, w_ref, hid_ref,
    stat_ref, a_ref, acc_ref, act_ref,
):
    strip = lax.axis_index("band") >> 1
    sums = sum0_ref[...] + sum1_ref[...] + sum2_ref[...] + sum3_ref[...]
    center, factor = center_factor(sums * (1.0 / members))
    for i in range(12):
        rows = slice(64 * i, 64 * i + 64)
        act = silu((mid_ref[rows, :] - center) * factor)
        if i == 0:
            act = act * jnp.where(strip > 0, 1.0, 0.0)
        elif i == 11:
            act = act * jnp.where(strip < 3, 1.0, 0.0)
        act_ref[rows, :] = act
    put_pairs(a_ref, act_ref, 5)
    multiply(acc_ref, a_ref, w_ref, 320)
    total = jnp.zeros((8, 320), F32)
    square = jnp.zeros((8, 320), F32)
    hid_ref[...] = lift(own_ref[...], w_in_ref[...])
    for i in range(10):
        rows = slice(64 * i, 64 * i + 64)
        if i % 2 == 0:
            pair = shifted_pair(acc_ref, i // 2)
        out = hid_ref[rows, :] + pair[i % 2]
        hid_ref[rows, :] = out
        folded = out.reshape(8, 8, 320)
        total += jnp.sum(folded, axis=0)
        square += jnp.sum(folded * folded, axis=0)
    write_sums(stat_ref, total, square)


def project_kernel(
    members, last, hid_ref, sum0_ref, sum1_ref, sum2_ref, sum3_ref, own_ref, w_out_ref, fold_ref,
    coef_ref, out_ref,
):
    sums = sum0_ref[...] + sum1_ref[...] + sum2_ref[...] + sum3_ref[...]
    center, factor = center_factor(sums * (1.0 / members))
    if last:
        low = lax.axis_index("band") & 1
        hidden = hid_ref[pl.ds(pl.multiple_of(low * 320, 64), 320), :]
        both = own_ref[...]
        own = jnp.where(low == 0, both[:, 0:320], both[:, 320:640])
    else:
        hidden = hid_ref[...]
        own = own_ref[...]
    act = silu((hidden - center) * factor)
    w_out = jnp.concatenate([w_out_ref[...], w_out_ref[...] * 0.0], axis=0)
    from_hidden = product(w_out, hidden, ((1,), (1,)))
    from_act = product(fold_ref[...], act, ((1,), (1,)))
    local = from_hidden[0:4] + from_act[0:4]
    ratio = coef_ref[0:1, 0:1]
    noise = coef_ref[1:2, 0:1]
    out_ref[0:4] = ratio * own + noise * local
    out_ref[4:8] = jnp.broadcast_to(noise, (4, out_ref.shape[1]))
    even = (lax.axis_index("level") & 1) == 0 if last else True
    out_ref[8:12] = jnp.where(even, from_act[4:8], from_act[8:12])
    out_ref[12:16] = jnp.where(even, from_act[8:12], from_act[4:8])


def merge_kernel(parts_ref, one_ref, two_ref, fresh_ref, own_ref):
    moved = one_ref[0:4] + one_ref[4:8] * (two_ref[...] + parts_ref[12:16])
    own_ref[...] = jnp.where(lax.axis_index("level") == 0, fresh_ref[...], moved)


def finish_kernel(parts_ref, core_ref, chip_ref, out_ref):
    own = parts_ref[0:4] + parts_ref[4:8] * (core_ref[...] + chip_ref[...])
    for r in range(5):
        out_ref[0, r] = own[:, 64 * r : 64 * r + 64]


SMEM = pl.BlockSpec(memory_space=pltpu.SMEM)
VMEM = pl.BlockSpec(memory_space=pltpu.VMEM)
ANY = pl.BlockSpec(memory_space=pl.ANY)
LIMIT = 20 * 1024 * 1024


def conv_call(kernel, operands, rows_in, rows_out, name):
    return pl.pallas_call(
        kernel,
        in_specs=[VMEM] * len(operands),
        out_specs=[VMEM, VMEM],
        out_shape=[
            jax.ShapeDtypeStruct((rows_out * 64, 320), F32),
            jax.ShapeDtypeStruct((2, 320), F32),
        ],
        scratch_shapes=[
            pltpu.VMEM((4, rows_out * 32, 1024), BF16),
            pltpu.VMEM((4, rows_out * 32 + 16, 960), F32),
            pltpu.VMEM((rows_in * 64, 320), F32),
        ],
        compiler_params=pltpu.CompilerParams(vmem_limit_bytes=LIMIT),
        cost_estimate=pl.CostEstimate(
            flops=4 * rows_out * 64 * 2880 * 320,
            bytes_accessed=4_000_000,
            transcendentals=rows_in * 64 * 320,
        ),
        name=name,
    )(*operands)


def call(kernel, in_specs, shapes, operands, name, cost=None):
    return pl.pallas_call(
        kernel,
        in_specs=in_specs,
        out_specs=[VMEM] * len(shapes),
        out_shape=[jax.ShapeDtypeStruct(shape, F32) for shape in shapes],
        compiler_params=pltpu.CompilerParams(vmem_limit_bytes=LIMIT),
        cost_estimate=cost,
        name=name,
    )(*operands)


def around_strip(value):
    bands = lax.axis_size("band")
    return [value] + [
        lax.ppermute(value, "band", [(i, i ^ (2 * flip)) for i in range(bands)])
        for flip in (1, 3, 2)
    ]


def swap_slots(to_core, to_chip):
    levels = lax.axis_size("level")
    across = [(i, i + 1) for i in range(1, levels - 1, 2)]
    across = across + [(j, i) for i, j in across]
    from_core = lax.ppermute(to_core, "level", [(i, i ^ 1) for i in range(levels)])
    from_chip = lax.ppermute(to_chip, "level", across)
    return from_core, from_chip


def on_device(latents, timesteps, fresh, w_in, conv_first, conv_second, w_time, temporal, w_out):
    levels = lax.axis_size("level")
    positions = latents.shape[2] * latents.shape[3]
    members = float(positions * lax.axis_size("band"))
    out_rows = w_out.T
    harmonic = harmonics(timesteps, w_time.shape[0])
    plan = np.zeros((8, 128), np.float32)
    plan.reshape(-1)[:NSTEPS] = noise_plan()
    plan = jnp.asarray(plan)
    spread, step = call(
        spread_kernel, [SMEM, VMEM, ANY], [(8, 8, positions), (1, 128)],
        (timesteps, jnp.concatenate([latents, fresh]).transpose(0, 2, 1, 3), harmonic),
        "spread", pl.CostEstimate(flops=8_000_000_000, bytes_accessed=40_000, transcendentals=0),
    )
    frame = lax.all_to_all(spread, "band", 0, 0, tiled=True)
    *pieces, new, coef, embedded, first_ready = setup(
        setup_kernel, [VMEM] * 6, [*[(4, 2 * positions)] * 5, (2, 128), (1, 320)],
        (frame, step, plan, harmonic, w_time, conv_first), "setup_first",
    )
    for iteration in range(ITERS):
        last = iteration + 1 == ITERS
        middle, stats = conv_call(
            functools.partial(conv1_kernel, members),
            (*pieces, w_in, embedded, first_ready),
            14, 12, "conv_one",
        )
        if iteration == 0:
            folded, second_ready = setup(
                setup_second_kernel, [ANY] + [VMEM] * 3, [(16, 320)],
                (stats, out_rows, temporal, conv_second), "setup_second",
            )
        hidden, stats = conv_call(
            functools.partial(conv2_kernel, members),
            (middle, *around_strip(stats), pieces[0], w_in, second_ready),
            12, 10, "conv_two",
        )
        width = positions if last else 2 * positions
        (parts,) = call(
            functools.partial(project_kernel, members, last), [VMEM] * 9, [(16, width)],
            (hidden, *around_strip(stats), pieces[0], out_rows, folded, coef), "project",
        )
        if last:
            (out,) = call(
                finish_kernel, [VMEM] * 3, [(1, 5, 4, 64)],
                (parts, *swap_slots(parts[8:12], parts[12:16])), "finish",
            )
        else:
            one = lax.ppermute(parts[0:8], "level", [(i, i + 1) for i in range(levels - 1)])
            two = lax.ppermute(parts[8:12], "level", [(i, i + 2) for i in range(levels - 2)])
            (own,) = call(
                merge_kernel, [VMEM] * 4, [(4, width)], (parts, one, two, new), "merge"
            )
            pieces = around_strip(own)
    return out.transpose(0, 2, 1, 3)


def solution(mesh):
    placed = (
        P("level", None, "band", None),
        P("level"),
        P(None, None, "band", None),
        P(),
        P(),
        P(),
        P(),
        P(),
        P(),
    )
    return jax.shard_map(
        on_device,
        mesh=mesh,
        in_specs=placed,
        out_specs=P("level", None, "band", None),
        check_vma=False,
    )
```

```python
import functools
import math

import jax
import jax.numpy as jnp
import numpy as np
from jax import lax
from jax.experimental import pallas as pl
from jax.experimental.pallas import tpu as pltpu
from jax.sharding import PartitionSpec as P

GROUPS = 32
ITERS = 2
NSTEPS = 1000
STRIDE = 16

EPSILON = 1e-05
HIGHEST = lax.Precision.HIGHEST
BF16 = jnp.bfloat16
F32 = jnp.float32


def noise_plan():
    position = np.arange(NSTEPS, dtype=np.float64)
    root_beta = math.sqrt(0.00085) + position / (NSTEPS - 1) * (
        math.sqrt(0.012) - math.sqrt(0.00085)
    )
    return np.cumprod(1.0 - root_beta * root_beta).astype(np.float32)


def harmonics(step_ids, width):
    half_width = width // 2
    frequency = jnp.exp(-math.log(10000.0) * jnp.arange(half_width, dtype=F32) / half_width)
    angles = step_ids.astype(F32)[:, None] * frequency[None, :]
    return jnp.concatenate([jnp.cos(angles), jnp.sin(angles)], axis=1)


def halves(v):
    hi = v.astype(BF16)
    return hi, (v - hi.astype(F32)).astype(BF16)


def thirds(v):
    one = v.astype(BF16).astype(F32)
    two = (v - one).astype(BF16).astype(F32)
    three = ((v - one) - two).astype(BF16).astype(F32)
    return one, two, three


def silu(v):
    return v / (1.0 + jnp.exp(-v))


def group_mean(rows):
    channels = rows.shape[1]
    per_group = channels // GROUPS
    one, two, three = thirds(rows)
    stacked = jnp.concatenate([one, two, three, one * 0.0], axis=0).astype(BF16)
    shape = (channels, channels)
    factor = (1 << 16) // per_group + 1
    here = (lax.broadcasted_iota(jnp.int32, shape, 0) * factor) >> 16
    there = (lax.broadcasted_iota(jnp.int32, shape, 1) * factor) >> 16
    member = jnp.where(here == there, 1.0, 0.0).astype(BF16)
    total = jnp.dot(stacked, member, preferred_element_type=F32)
    return (total[0:2] + total[2:4] + total[4:6]) * (1.0 / per_group)


def center_factor(means):
    grouped = group_mean(means)
    center = grouped[0:1]
    return center, lax.rsqrt(grouped[1:2] - center * center + EPSILON)


def lift(frame, w):
    f1, f2, f3 = thirds(frame)
    w1, w2, w3 = thirds(w)
    left = jnp.concatenate([f1, f1, f2, f1, f2, f3], axis=0).astype(BF16)
    right = jnp.concatenate([w1, w2, w1, w3, w2, w1], axis=0).astype(BF16)
    return lax.dot_general(left, right, (((0,), (0,)), ((), ())), preferred_element_type=F32)


def put_left(a_ref, j, rows, act):
    hi, lo = halves(act)
    a_ref[j, rows, 0:256] = hi[:, 0:256]
    a_ref[j, rows, 256:512] = lo[:, 0:256]
    a_ref[j, rows, 512:768] = hi[:, 0:256]
    a_ref[j, rows, 768:896] = jnp.concatenate([hi[:, 256:320], lo[:, 256:320]], axis=1)
    a_ref[j, rows, 896:1024] = jnp.concatenate([hi[:, 256:320], hi[:, 256:320] * 0.0], axis=1)


def put_pairs(a_ref, act_ref, pairs):
    for t in range(pairs):
        d0, d1, d2, d3 = (act_ref[128 * t + 64 * i : 128 * t + 64 * i + 64, :] for i in range(4))
        for j, mixed in enumerate((d0 - d2, d1 + d2, d2 - d1, d1 - d3)):
            put_left(a_ref, j, slice(64 * t, 64 * t + 64), mixed)


def put_right(b_ref, raw_ref):
    for k in range(5):
        taps = []
        for c in range(3):
            g0, g1, g2 = (raw_ref[r, c, 64 * k : 64 * k + 64, :] for r in range(3))
            ends = (g0 + g2) * 0.5
            middle = g1 * 0.5
            taps.append((g0, ends + middle, ends - middle, g2))
        for j in range(4):
            hi, lo = zip(*[halves(tap[j]) for tap in taps])
            if k < 4:
                places = ((64 * k, hi), (256 + 64 * k, hi), (512 + 64 * k, lo))
            else:
                places = ((768, hi), (832, hi), (896, lo))
            for at, part in places:
                for c in range(3):
                    b_ref[j, at : at + 64, 256 * c : 256 * c + 256] = part[c][:, 0:256]
                b_ref[j, at : at + 64, 768:896] = jnp.concatenate(
                    [part[0][:, 256:320], part[1][:, 256:320]], axis=1
                )
                b_ref[j, at : at + 64, 896:960] = part[2][:, 256:320]
    for j in range(4):
        b_ref[j, 960:1024, :] = jnp.zeros((64, 960), BF16)


def product(left, right, dims):
    l_hi, l_lo = halves(left)
    r_hi, r_lo = halves(right)
    n = left.shape[0]
    both = lax.dot_general(
        jnp.concatenate([l_hi, l_lo], axis=0), r_hi, (dims, ((), ())), preferred_element_type=F32
    )
    rest = lax.dot_general(l_hi, r_lo, (dims, ((), ())), preferred_element_type=F32)
    return both[0:n] + both[n:] + rest


def spread_kernel(
    steps_ref, frames_ref, harmonic_ref, spread_ref, step_ref
):
    rows = [
        jnp.concatenate([frames_ref[i, r] for r in range(5)], axis=1) for i in range(2)
    ]
    both = jnp.concatenate(rows, axis=0)
    spread_ref[...] = jnp.broadcast_to(both[None], spread_ref.shape)
    step_ref[...] = jnp.full(step_ref.shape, steps_ref[0].astype(F32), F32)


def setup_kernel(
    frame_ref, step_ref, plan_ref, harmonic_ref, time_ref, raw_ref, own_ref, flip1_ref, flip3_ref,
    flip2_ref, new_ref, coef_ref, emb_ref, first_ref,
):
    strip = lax.axis_index("band") >> 1

    def piece(flip, row):
        at = 2 * (strip ^ flip)
        return jnp.concatenate(
            [frame_ref[at, row : row + 4, :], frame_ref[at + 1, row : row + 4, :]], axis=1
        )

    for ref, flip in ((own_ref, 0), (flip1_ref, 1), (flip3_ref, 3), (flip2_ref, 2)):
        ref[...] = piece(flip, 0)
    new_ref[...] = piece(0, 4)
    step = step_ref[...].astype(jnp.int32)
    plan = plan_ref[...]
    place = lax.broadcasted_iota(jnp.int32, plan.shape, 0) * 128 + lax.broadcasted_iota(
        jnp.int32, plan.shape, 1
    )

    def at(i):
        return jnp.sum(
            jnp.sum(jnp.where(place == i, plan, 0.0), axis=0, keepdims=True), axis=1, keepdims=True
        )

    now = at(step)
    prev = at(step - STRIDE)
    ratio = jnp.sqrt(prev) / jnp.sqrt(now)
    noise = jnp.sqrt(1.0 - prev) - ratio * jnp.sqrt(1.0 - now)
    coef_ref[0:1] = jnp.broadcast_to(ratio, (1, 128))
    coef_ref[1:2] = jnp.broadcast_to(noise, (1, 128))
    put_right(first_ref, raw_ref)
    harmonic = jnp.broadcast_to(harmonic_ref[...], (8, 320))
    emb_ref[...] = silu(product(harmonic, time_ref[...], ((1,), (0,)))[0:1])


def setup_second_kernel(after_ref, w_out_ref, temporal_ref, raw_ref, fold_ref, second_ref):
    put_right(second_ref, raw_ref)
    w_out = jnp.concatenate([w_out_ref[...], w_out_ref[...] * 0.0], axis=0)
    for row, tap in enumerate((1, 0, 2)):
        fold = product(w_out, temporal_ref[tap], ((1,), (1,)))
        fold_ref[4 * row : 4 * row + 4] = fold[0:4]
    fold_ref[12:16] = jnp.zeros((4, 320), F32)


def setup(kernel, specs, shapes, operands, name):
    return pl.pallas_call(
        kernel,
        in_specs=specs,
        out_specs=[VMEM] * (len(shapes) + 1),
        out_shape=[
            *[jax.ShapeDtypeStruct(shape, F32) for shape in shapes],
            jax.ShapeDtypeStruct((4, 1024, 960), BF16),
        ],
        compiler_params=pltpu.CompilerParams(vmem_limit_bytes=LIMIT),
        cost_estimate=pl.CostEstimate(flops=0, bytes_accessed=10_000_000, transcendentals=0),
        name=name,
    )(*operands)


def multiply(acc_ref, a_ref, b_ref, count):
    for j in range(4):
        for lo, hi in ((0, 256), (256, 512), (512, 768), (768, 960)):
            acc_ref[j, 8 : 8 + count, lo:hi] = jnp.dot(
                a_ref[j], b_ref[j, :, lo:hi], preferred_element_type=F32
            )


def shifted_pair(acc_ref, t):
    base = 8 + 64 * t
    column = lax.broadcasted_iota(jnp.int32, (64, 1), 0)
    first = column > 0
    last = column < 63

    def tap(shift, lo, hi):
        m1, m2, m3, m4 = (acc_ref[j, base + shift : base + shift + 64, lo:hi] for j in range(4))
        return (m1 + (m2 + m3), (m2 - m3) - m4)

    out = []
    for at, width in ((0, 256), (768, 64)):
        left = tap(-1, at, at + width)
        here = tap(0, at + width, at + 2 * width)
        right = tap(1, at + 2 * width, at + 3 * width)
        out.append(
            [
                jnp.where(first, left[i], 0.0) + here[i] + jnp.where(last, right[i], 0.0)
                for i in range(2)
            ]
        )
    return [jnp.concatenate([out[0][i], out[1][i]], axis=1) for i in range(2)]


def write_sums(stat_ref, total, square):
    stat_ref[...] = jnp.concatenate(
        [jnp.sum(total, axis=0, keepdims=True), jnp.sum(square, axis=0, keepdims=True)], axis=0
    )


def conv1_kernel(
    members, own_ref, flip1_ref, flip3_ref, flip2_ref, w_in_ref, emb_ref, w_ref, mid_ref, stat_ref,
    a_ref, acc_ref, lift_ref,
):
    strip = lax.axis_index("band") >> 1
    pieces = [ref[...] for ref in (own_ref, flip1_ref, flip3_ref, flip2_ref)]
    w = w_in_ref[...]
    average = 1.0 / members
    mean = jnp.sum(sum(pieces), axis=1, keepdims=True) * average
    mean = jnp.sum(mean * w, axis=0, keepdims=True)
    square = jnp.zeros_like(mean)
    for j in range(4):
        moment = sum(piece * piece[j : j + 1] for piece in pieces)
        moment = jnp.sum(moment, axis=1, keepdims=True) * average
        square += w[j : j + 1] * jnp.sum(moment * w, axis=0, keepdims=True)
    center, factor = center_factor(jnp.concatenate([mean, square], axis=0))
    odd = (strip & 1) == 1
    before = jnp.where(odd, pieces[1][:, 512:640], pieces[2][:, 512:640])
    after = jnp.where(odd, pieces[2][:, 0:128], pieces[1][:, 0:128])
    around = jnp.concatenate([before, pieces[0], after], axis=1)
    lift_ref[...] = lift(around, w)
    for i in range(14):
        rows = slice(64 * i, 64 * i + 64)
        act = silu((lift_ref[rows, :] - center) * factor)
        if i < 2:
            act = act * jnp.where(strip > 0, 1.0, 0.0)
        elif i >= 12:
            act = act * jnp.where(strip < 3, 1.0, 0.0)
        lift_ref[rows, :] = act
    put_pairs(a_ref, lift_ref, 6)
    multiply(acc_ref, a_ref, w_ref, 384)
    total = jnp.zeros((8, 320), F32)
    square = jnp.zeros((8, 320), F32)
    for i in range(12):
        if i % 2 == 0:
            pair = shifted_pair(acc_ref, i // 2)
        out = pair[i % 2] + emb_ref[...]
        mid_ref[64 * i : 64 * i + 64, :] = out
        if 1 <= i <= 10:
            folded = out.reshape(8, 8, 320)
            total += jnp.sum(folded, axis=0)
            square += jnp.sum(folded * folded, axis=0)
    write_sums(stat_ref, total, square)


def conv2_kernel(
    members, mid_ref, sum0_ref, sum1_ref, sum2_ref, sum3_ref, own_ref, w_in_ref, w_ref, hid_ref,
    stat_ref, a_ref, acc_ref, act_ref,
):
    strip = lax.axis_index("band") >> 1
    sums = sum0_ref[...] + sum1_ref[...] + sum2_ref[...] + sum3_ref[...]
    center, factor = center_factor(sums * (1.0 / members))
    for i in range(12):
        rows = slice(64 * i, 64 * i + 64)
        act = silu((mid_ref[rows, :] - center) * factor)
        if i == 0:
            act = act * jnp.where(strip > 0, 1.0, 0.0)
        elif i == 11:
            act = act * jnp.where(strip < 3, 1.0, 0.0)
        act_ref[rows, :] = act
    put_pairs(a_ref, act_ref, 5)
    multiply(acc_ref, a_ref, w_ref, 320)
    total = jnp.zeros((8, 320), F32)
    square = jnp.zeros((8, 320), F32)
    hid_ref[...] = lift(own_ref[...], w_in_ref[...])
    for i in range(10):
        rows = slice(64 * i, 64 * i + 64)
        if i % 2 == 0:
            pair = shifted_pair(acc_ref, i // 2)
        out = hid_ref[rows, :] + pair[i % 2]
        hid_ref[rows, :] = out
        folded = out.reshape(8, 8, 320)
        total += jnp.sum(folded, axis=0)
        square += jnp.sum(folded * folded, axis=0)
    write_sums(stat_ref, total, square)


def base_kernel(last, hid_ref, w_out_ref, base_ref):
    if last:
        low = lax.axis_index("band") & 1
        hidden = hid_ref[pl.ds(pl.multiple_of(low * 320, 64), 320), :]
    else:
        hidden = hid_ref[...]
    w_out = jnp.concatenate([w_out_ref[...], w_out_ref[...] * 0.0], axis=0)
    base_ref[...] = product(w_out, hidden, ((1,), (1,)))


def project_kernel(
    members, last, hid_ref, sum0_ref, sum1_ref, sum2_ref, sum3_ref, own_ref, base_ref, fold_ref,
    coef_ref, out_ref,
):
    sums = sum0_ref[...] + sum1_ref[...] + sum2_ref[...] + sum3_ref[...]
    center, factor = center_factor(sums * (1.0 / members))
    if last:
        low = lax.axis_index("band") & 1
        hidden = hid_ref[pl.ds(pl.multiple_of(low * 320, 64), 320), :]
        both = own_ref[...]
        own = jnp.where(low == 0, both[:, 0:320], both[:, 320:640])
    else:
        hidden = hid_ref[...]
        own = own_ref[...]
    act = silu((hidden - center) * factor)
    from_act = product(fold_ref[...], act, ((1,), (1,)))
    local = base_ref[0:4] + from_act[0:4]
    ratio = coef_ref[0:1, 0:1]
    noise = coef_ref[1:2, 0:1]
    out_ref[0:4] = ratio * own + noise * local
    out_ref[4:8] = jnp.broadcast_to(noise, (4, out_ref.shape[1]))
    even = (lax.axis_index("level") & 1) == 0 if last else True
    out_ref[8:12] = jnp.where(even, from_act[4:8], from_act[8:12])
    out_ref[12:16] = jnp.where(even, from_act[8:12], from_act[4:8])


def merge_kernel(parts_ref, one_ref, two_ref, fresh_ref, own_ref):
    moved = one_ref[0:4] + one_ref[4:8] * (two_ref[...] + parts_ref[12:16])
    own_ref[...] = jnp.where(lax.axis_index("level") == 0, fresh_ref[...], moved)


def finish_kernel(parts_ref, core_ref, chip_ref, out_ref):
    own = parts_ref[0:4] + parts_ref[4:8] * (core_ref[...] + chip_ref[...])
    for r in range(5):
        out_ref[0, r] = own[:, 64 * r : 64 * r + 64]


SMEM = pl.BlockSpec(memory_space=pltpu.SMEM)
VMEM = pl.BlockSpec(memory_space=pltpu.VMEM)
ANY = pl.BlockSpec(memory_space=pl.ANY)
LIMIT = 20 * 1024 * 1024


def conv_call(kernel, operands, rows_in, rows_out, name):
    return pl.pallas_call(
        kernel,
        in_specs=[VMEM] * len(operands),
        out_specs=[VMEM, VMEM],
        out_shape=[
            jax.ShapeDtypeStruct((rows_out * 64, 320), F32),
            jax.ShapeDtypeStruct((2, 320), F32),
        ],
        scratch_shapes=[
            pltpu.VMEM((4, rows_out * 32, 1024), BF16),
            pltpu.VMEM((4, rows_out * 32 + 16, 960), F32),
            pltpu.VMEM((rows_in * 64, 320), F32),
        ],
        compiler_params=pltpu.CompilerParams(vmem_limit_bytes=LIMIT),
        cost_estimate=pl.CostEstimate(
            flops=4 * rows_out * 64 * 2880 * 320,
            bytes_accessed=4_000_000,
            transcendentals=rows_in * 64 * 320,
        ),
        name=name,
    )(*operands)


def call(kernel, in_specs, shapes, operands, name, cost=None):
    return pl.pallas_call(
        kernel,
        in_specs=in_specs,
        out_specs=[VMEM] * len(shapes),
        out_shape=[jax.ShapeDtypeStruct(shape, F32) for shape in shapes],
        compiler_params=pltpu.CompilerParams(vmem_limit_bytes=LIMIT),
        cost_estimate=cost,
        name=name,
    )(*operands)


def around_strip(value):
    bands = lax.axis_size("band")
    return [value] + [
        lax.ppermute(value, "band", [(i, i ^ (2 * flip)) for i in range(bands)])
        for flip in (1, 3, 2)
    ]


def swap_slots(to_core, to_chip):
    levels = lax.axis_size("level")
    across = [(i, i + 1) for i in range(1, levels - 1, 2)]
    across = across + [(j, i) for i, j in across]
    from_core = lax.ppermute(to_core, "level", [(i, i ^ 1) for i in range(levels)])
    from_chip = lax.ppermute(to_chip, "level", across)
    return from_core, from_chip


def on_device(latents, timesteps, fresh, w_in, conv_first, conv_second, w_time, temporal, w_out):
    levels = lax.axis_size("level")
    positions = latents.shape[2] * latents.shape[3]
    members = float(positions * lax.axis_size("band"))
    out_rows = w_out.T
    harmonic = harmonics(timesteps, w_time.shape[0])
    plan = np.zeros((8, 128), np.float32)
    plan.reshape(-1)[:NSTEPS] = noise_plan()
    plan = jnp.asarray(plan)
    spread, step = call(
        spread_kernel, [SMEM, VMEM, ANY], [(8, 8, positions), (1, 128)],
        (timesteps, jnp.concatenate([latents, fresh]).transpose(0, 2, 1, 3), harmonic),
        "spread", pl.CostEstimate(flops=8_000_000_000, bytes_accessed=40_000, transcendentals=0),
    )
    frame = lax.all_to_all(spread, "band", 0, 0, tiled=True)
    *pieces, new, coef, embedded, first_ready = setup(
        setup_kernel, [VMEM] * 6, [*[(4, 2 * positions)] * 5, (2, 128), (1, 320)],
        (frame, step, plan, harmonic, w_time, conv_first), "setup_first",
    )
    for iteration in range(ITERS):
        last = iteration + 1 == ITERS
        middle, stats = conv_call(
            functools.partial(conv1_kernel, members),
            (*pieces, w_in, embedded, first_ready),
            14, 12, "conv_one",
        )
        if iteration == 0:
            folded, second_ready = setup(
                setup_second_kernel, [ANY] + [VMEM] * 3, [(16, 320)],
                (stats, out_rows, temporal, conv_second), "setup_second",
            )
        hidden, stats = conv_call(
            functools.partial(conv2_kernel, members),
            (middle, *around_strip(stats), pieces[0], w_in, second_ready),
            12, 10, "conv_two",
        )
        width = positions if last else 2 * positions
        (base,) = call(
            functools.partial(base_kernel, last), [VMEM] * 2, [(8, width)], (hidden, out_rows),
            "base", pl.CostEstimate(flops=20_000_000, bytes_accessed=1_000_000, transcendentals=0),
        )
        (parts,) = call(
            functools.partial(project_kernel, members, last), [VMEM] * 9, [(16, width)],
            (hidden, *around_strip(stats), pieces[0], base, folded, coef), "project",
        )
        if last:
            (out,) = call(
                finish_kernel, [VMEM] * 3, [(1, 5, 4, 64)],
                (parts, *swap_slots(parts[8:12], parts[12:16])), "finish",
            )
        else:
            one = lax.ppermute(parts[0:8], "level", [(i, i + 1) for i in range(levels - 1)])
            two = lax.ppermute(parts[8:12], "level", [(i, i + 2) for i in range(levels - 2)])
            (own,) = call(
                merge_kernel, [VMEM] * 4, [(4, width)], (parts, one, two, new), "merge"
            )
            pieces = around_strip(own)
    return out.transpose(0, 2, 1, 3)


def solution(mesh):
    placed = (
        P("level", None, "band", None),
        P("level"),
        P(None, None, "band", None),
        P(),
        P(),
        P(),
        P(),
        P(),
        P(),
    )
    return jax.shard_map(
        on_device,
        mesh=mesh,
        in_specs=placed,
        out_specs=P("level", None, "band", None),
        check_vma=False,
    )
```
